32 devices in a mesh: dp: 8 (over y, x, core), tensor: 4 (over z).
Axes of the slice: x: 2, y: 2, z: 4, core: 2. Of those that a mesh axis runs over, the one named last changes fastest.
Arguments:
- teacher_hidden: bfloat16 [1024, 4096], P('dp'), may hold values from -6 to 6
- student_hidden: bfloat16 [1024, 2048], P('dp'), may hold values from -6 to 6
- target_ids: int32 [1024], P('dp'), may hold values from 0 to 64127
- teacher_head: bfloat16 [4096, 65536], P(None, ('dp', 'tensor')), may hold values from -1 to 1
- student_head: bfloat16 [2048, 65536], P(None, ('dp', 'tensor')), may hold values from -1 to 1
Outputs:
- head_grad: float32 [2048, 65536], P(None, ('dp', 'tensor'))
- input_grad: float32 [1024, 2048], P('dp', 'tensor')
The draws below stay inside these ranges and needn't reach their ends.
All inputs are finite; a program needn't handle non-finite values.
Results may differ from the reference program's by a relative error of at most 0.0065.
Values may be sent and summed in bfloat16 or wider, within the bound.
A program may use at most 128 MiB of HBM per device.

```python
import math
import jax
import jax.numpy as jnp
import numpy as np
from jax import lax

DT = 4096
DS = 2048
VOCAB = 64128
PADDED = 65536
TOKENS = 1024


def column_vectors(head_key, depth, indices):
    scale = 4.0 / jnp.sqrt(jnp.float32(depth))
    one_column = lambda index: jax.random.normal(jax.random.fold_in(head_key, index), (depth,), jnp.float32)
    return jax.vmap(one_column)(indices) * scale


def head_matrix(key, salt, depth):
    head_key = jax.random.fold_in(key, salt)
    columns = column_vectors(head_key, depth, jnp.arange(PADDED, dtype=jnp.int32))
    return jnp.clip(columns.T, -1.0, 1.0).astype(jnp.bfloat16)


def hidden_rows(key, salt, depth):
    drawn_rows = jnp.clip(jax.random.normal(jax.random.fold_in(key, salt), (TOKENS, depth), jnp.float32), -6.0, 6.0)
    return drawn_rows.astype(jnp.bfloat16)


def draw_teacher_head(key, part):
    return head_matrix(key, 101, DT)


def draw_student_head(key, part):
    return head_matrix(key, 202, DS)


def draw_teacher_hidden(key, part):
    return hidden_rows(key, 303, DT)


def draw_student_hidden(key, part):
    return hidden_rows(key, 404, DS)


def plant(drawn, own_key, least, top_value):
    longest = drawn.shape.index(max(drawn.shape))
    spots = []
    for shift in (0, 1):
        where = [jax.random.randint(jax.random.fold_in(own_key, axis), (), 0, length) for axis, length in enumerate(drawn.shape)]
        where[longest] = (where[longest] + shift) % drawn.shape[longest]
        spots.append(tuple(where))
    return drawn.at[spots[0]].set(least).at[spots[1]].set(top_value)


def rank_table(number_of, slope):
    portions = [(1 << 20) // math.isqrt(standing ** slope) + 1 for standing in range(1, number_of + 1)]
    scale = 1 + sum(portions) // (1 << 30)
    return np.cumsum(np.array([max(1, weight // scale) for weight in portions]))


def ranked_ids(stream_key, extent, count, slope):
    table = rank_table(count, slope)
    pick = jax.random.randint(jax.random.fold_in(stream_key, 1), extent, 0, int(table[count - 1]))
    rank = jnp.searchsorted(jnp.asarray(table, jnp.int32), pick, side="right")
    return jax.random.permutation(jax.random.fold_in(stream_key, 2), count)[rank].astype(jnp.int32)


def setup_inputs(seed: int = 0) -> dict:
    streams_of = jax.random.split(jax.random.key(seed), 6)
    teacher_hidden = draw_teacher_hidden(jax.random.fold_in(streams_of[5], 71), 0)
    student_hidden = draw_student_hidden(jax.random.fold_in(streams_of[5], 71), 0)
    target_ids = plant(ranked_ids(streams_of[2], (TOKENS,), VOCAB, 2), jax.random.fold_in(streams_of[2], 3), 0, VOCAB - 1).astype(jnp.int32)
    teacher_head = draw_teacher_head(jax.random.fold_in(streams_of[5], 71), 0)
    student_head = draw_student_head(jax.random.fold_in(streams_of[5], 71), 0)
    return {"teacher_hidden": teacher_hidden, "student_hidden": student_hidden, "target_ids": target_ids, "teacher_head": teacher_head, "student_head": student_head}


def softmax_rows(logits):
    peak = jnp.max(logits, axis=1, keepdims=True)
    expo = jnp.exp(logits - peak)
    return expo / jnp.sum(expo, axis=1, keepdims=True)


def reference(teacher_hidden, student_hidden, target_ids, teacher_head, student_head):
    columns = jnp.arange(PADDED, dtype=jnp.int32)
    is_real = (columns < VOCAB)[None, :]
    teacher_logits = jnp.where(is_real, jnp.dot(teacher_hidden, teacher_head, preferred_element_type=jnp.float32), jnp.float32(-1e30))
    student_logits = jnp.where(is_real, jnp.dot(student_hidden, student_head, preferred_element_type=jnp.float32), jnp.float32(-1e30))
    teacher_probs = softmax_rows(teacher_logits)
    student_probs = softmax_rows(student_logits)
    onehot = (target_ids[:, None] == columns[None, :]).astype(jnp.float32)
    logit_grad = (2.0 * student_probs - teacher_probs - onehot).astype(jnp.bfloat16)
    head_grad = lax.dot_general(student_hidden, logit_grad, (((0,), (0,)), ((), ())), preferred_element_type=jnp.float32)
    input_grad = lax.dot_general(logit_grad, student_head, (((1,), (1,)), ((), ())), preferred_element_type=jnp.float32)
    return head_grad, input_grad
```

```python
import functools

import jax
import jax.numpy as jnp
from jax import lax
from jax.experimental import pallas as pl
from jax.experimental.pallas import tpu as pltpu
from jax.sharding import PartitionSpec as P

VOCAB = 64128


def body(teacher_hidden, student_hidden, target_ids, teacher_head, student_head):
    width_cols = teacher_head.shape[1]
    first_col = (
        lax.axis_index("dp") * lax.axis_size("tensor") + lax.axis_index("tensor")
    ) * width_cols
    columns = first_col + lax.iota(jnp.int32, width_cols)
    is_real = (columns < VOCAB)[None, :]
    teacher_logits = jnp.dot(
        lax.all_gather(teacher_hidden, "dp", axis=0, tiled=True),
        teacher_head,
        preferred_element_type=jnp.float32,
    )
    teacher_logits = jnp.where(is_real, teacher_logits, jnp.float32(-1e30))
    student_rows, all_targets = (
        lax.all_gather(student_hidden, "dp", axis=0, tiled=True),
        lax.all_gather(target_ids, "dp", axis=0, tiled=True),
    )
    student_logits = jnp.where(
        is_real,
        jnp.dot(student_rows, student_head, preferred_element_type=jnp.float32),
        jnp.float32(-1e30),
    )
    peaks = jnp.stack([jnp.max(teacher_logits, axis=1), jnp.max(student_logits, axis=1)])
    totals = jnp.stack(
        [
            jnp.sum(jnp.exp(teacher_logits - peaks[0][:, None]), axis=1),
            jnp.sum(jnp.exp(student_logits - peaks[1][:, None]), axis=1),
        ]
    )
    table = lax.all_gather(jnp.concatenate([peaks, totals]), ("dp", "tensor"), axis=0)
    top = jnp.max(table[:, :2], axis=0)
    teacher_total, student_total = jnp.sum(table[:, 2:] * jnp.exp(table[:, :2] - top), axis=0)
    teacher_expo = jnp.exp(teacher_logits - top[0][:, None])
    student_expo = jnp.exp(student_logits - top[1][:, None])
    teacher_probs = teacher_expo / teacher_total[:, None]
    student_probs = student_expo / student_total[:, None]
    onehot = (all_targets[:, None] == columns[None, :]).astype(jnp.float32)
    logit_grad = (2.0 * student_probs - teacher_probs - onehot).astype(jnp.bfloat16)
    head_grad = lax.dot_general(
        student_rows, logit_grad, (((0,), (0,)), ((), ())), preferred_element_type=jnp.float32
    )
    own_rows = lax.psum_scatter(
        lax.dot_general(
            logit_grad, student_head, (((1,), (1,)), ((), ())), preferred_element_type=jnp.float32
        ),
        "dp",
        scatter_dimension=0,
        tiled=True,
    )
    input_grad = lax.psum_scatter(own_rows, "tensor", scatter_dimension=1, tiled=True)
    return (head_grad, input_grad)


MESH = pl.DeviceIdType.MESH
PIECES = 3
SLOTS = 19


def as_column(row):
    return jnp.transpose(jnp.broadcast_to(row, (row.shape[1], row.shape[1])))[:, :1]


def as_row(column):
    return jnp.transpose(jnp.broadcast_to(column, (column.shape[0], column.shape[0])))[:1, :]


def kernel(
    n, nt, tile,
    teacher_in, student_in, ids_in, teacher_head, student_head,
    grad_out, rows_out, *refs,
):
    part_outs = refs[:nt]
    (
        t_rows, s_rows, ids, t_w, s_w, t_exp, s_exp,
        stats, stats_in, stats_mid, scale, pair_in, hop_in, plane_in,
        local_sem, out_sem, gather_send, gather_recv, ids_send, ids_recv,
        stats_send, stats_recv, pair_send, pair_recv, hop_send, hop_recv, plane_send, plane_recv,
    ) = refs[nt:]
    block = teacher_in.shape[0]
    pair = 2 * block
    quarter = block // 4
    width = t_w.shape[1]
    depth = s_w.shape[0]
    slab = t_w.shape[0] // 2
    features = depth // nt
    dp = lax.axis_index("dp")
    tz = lax.axis_index("tensor")
    chip, core = dp // 2, dp % 2
    parity = tz % 2

    def flip(value, bit):
        return value + bit - 2 * bit * ((value // bit) % 2)

    def other(d):
        out = chip
        for bit in (1, 2):
            if d & bit:
                out = flip(out, bit)
        return out

    sibling = (chip * 2 + 1 - core, tz)
    near = ((other(1) * 2 + core, tz), (other(2) * 2 + core, tz))
    mate = (dp, flip(tz, 1))
    blocks = [other(d) * 2 + core for d in range(4)]
    own = pl.ds(pl.multiple_of(dp * block, block), block)

    loads = [
        pltpu.make_async_copy(student_head, s_w, local_sem.at[0]),
        pltpu.make_async_copy(student_in, s_rows.at[own], local_sem.at[1]),
        pltpu.make_async_copy(teacher_in, t_rows.at[own], local_sem.at[2]),
        pltpu.make_async_copy(teacher_head.at[0:slab], t_w.at[0:slab], local_sem.at[3]),
        pltpu.make_async_copy(teacher_head.at[slab:], t_w.at[slab:], local_sem.at[4]),
    ]
    for load in loads:
        load.start()
    ids[dp] = jnp.broadcast_to(ids_in[...].astype(jnp.float32), (8, block))

    barrier = pltpu.get_barrier_semaphore()
    for k in range(1, n):
        pl.semaphore_signal(barrier, inc=1, device_id=(lax.rem(dp + k, n), tz), device_id_type=MESH)
    for k in range(1, nt):
        pl.semaphore_signal(barrier, inc=1, device_id=(dp, lax.rem(tz + k, nt)), device_id_type=MESH)
    pl.semaphore_wait(barrier, n - 1 + nt - 1)

    def remote(source, target, send, recv, device):
        return pltpu.make_async_remote_copy(
            src_ref=source, dst_ref=target, send_sem=send, recv_sem=recv,
            device_id=device, device_id_type=MESH,
        )

    pieces = ((student_in, s_rows, 0, depth), (teacher_in, t_rows, 0, slab), (teacher_in, t_rows, slab, slab))

    def at_quarter(i):
        return (i + parity * (3 - 2 * i)) * quarter

    first_half = parity * 2 * quarter
    second_half = (1 - parity) * 2 * quarter
    msgs = {}

    def send(p, slot):
        given, held, start, size = pieces[p]
        cols = pl.ds(start, size)
        x, y = near
        index, offset, count, device = {
            0: (0, at_quarter(0), quarter, x),
            1: (0, at_quarter(1), quarter, x),
            2: (2, at_quarter(0), quarter, x),
            3: (0, at_quarter(2), quarter, x),
            4: (0, at_quarter(0), quarter, y),
            5: (0, at_quarter(1), quarter, y),
            6: (1, at_quarter(1), quarter, y),
            7: (0, at_quarter(2), quarter, y),
            8: (1, at_quarter(0), quarter, mate),
            9: (2, at_quarter(0), quarter, mate),
            10: (3, at_quarter(0), quarter, mate),
            11: (3, at_quarter(1), quarter, mate),
            12: (0, 0, block, sibling),
            13: (1, first_half, 2 * quarter, sibling),
            14: (2, first_half, 2 * quarter, sibling),
            15: (3, first_half, 2 * quarter, sibling),
            16: (1, second_half, 2 * quarter, sibling),
            17: (2, second_half, 2 * quarter, sibling),
            18: (3, second_half, 2 * quarter, sibling),
        }[slot]
        target = pl.ds(pl.multiple_of(blocks[index] * block + offset, quarter), count)
        if index == 0:
            source = given.at[pl.ds(pl.multiple_of(offset, quarter), count), cols]
        else:
            source = held.at[target, cols]
        msgs[p, slot] = remote(
            source, held.at[target, cols], gather_send.at[p, slot], gather_recv.at[p, slot], device
        )
        msgs[p, slot].start()

    def arrived(p, *slots):
        for slot in slots:
            msgs[p, slot].wait_recv()

    for slot in (0, 4, 1, 5, 12):
        send(0, slot)
    for p in (1, 2):
        send(p, 12)
    id_msgs = []
    for k in range(1, n):
        id_msgs.append(
            remote(ids.at[dp], ids.at[dp], ids_send.at[k - 1], ids_recv.at[k - 1], (lax.rem(dp + k, n), tz))
        )
        id_msgs[-1].start()

    def step_a(p):
        arrived(p, 4)
        send(p, 2)
        send(p, 9)
        arrived(p, 0)
        send(p, 8)
        send(p, 3)
        send(p, 7)

    def step_b(p):
        arrived(p, 1)
        send(p, 6)
        if p + 1 < PIECES:
            for slot in (0, 4, 1, 5):
                send(p + 1, slot)
        send(p, 13)
        arrived(p, 5)
        send(p, 14)

    def step_c(p):
        arrived(p, 2)
        send(p, 10)

    def step_d(p):
        arrived(p, 6)
        send(p, 11)
        send(p, 15)
        arrived(p, 3, 8)
        send(p, 16)
        arrived(p, 7, 9)
        send(p, 17)

    def step_e(p):
        arrived(p, 10, 11)
        send(p, 18)

    first_col = (dp * nt + tz) * width
    tiles = width // tile

    def rows_of(d):
        return pl.ds(pl.multiple_of(other(d) * pair, pair), pair)

    def cols_of(j):
        return pl.ds(pl.multiple_of(j * tile, tile), tile)

    def column_ids(j):
        return first_col + j * tile + lax.broadcasted_iota(jnp.int32, (1, tile), 1)

    def exponential(held, cols):
        which, d, peak = held
        ref = (s_exp, t_exp)[which]
        e = jnp.exp(ref[rows_of(d), cols] - peak)
        ref[rows_of(d), cols] = e
        return jnp.sum(e, axis=1, keepdims=True)

    def record(held, total):
        which, d, peak = held
        for h in range(2):
            slot = pl.ds(other(d) * 2 + h, 1)
            stats[which, 0, slot, :] = as_row(peak[h * block : (h + 1) * block])
            stats[which, 1, slot, :] = as_row(total[h * block : (h + 1) * block])

    zero = jnp.zeros((pair, 1), jnp.float32)

    def logits(which, d, part, held):
        rows_ref, w_ref, z_ref = ((s_rows, s_w, s_exp), (t_rows, t_w, t_exp))[which]
        length = (depth, slab)[which]
        span = pl.ds(part * length, length)
        last = part == which
        rows = rows_of(d)

        def step(j, carry):
            peak, total = carry
            cols = cols_of(j)
            z = jnp.dot(rows_ref[rows, span], w_ref[span, cols], preferred_element_type=jnp.float32)
            if part:
                z = z + z_ref[rows, cols]
            if last:
                z = jnp.where(column_ids(j) < VOCAB, z, jnp.float32(-1e30))
                peak = jnp.maximum(peak, jnp.max(z, axis=1, keepdims=True))
            z_ref[rows, cols] = z
            if held is not None:
                total = total + exponential(held, cols)
            return peak, total

        peak, total = lax.fori_loop(0, tiles, step, (zero - jnp.inf, zero))
        if held is not None:
            record(held, total)
        return (which, d, peak) if last else None

    def settle(held):
        record(held, lax.fori_loop(0, tiles, lambda j, total: total + exponential(held, cols_of(j)), zero))

    stat_msgs = {}

    def stats_out(which, phase):
        for k in range(1, (n, nt)[phase]):
            slot = k - 1 + phase * (n - 1)
            device = ((lax.rem(dp + k, n), tz), (dp, lax.rem(tz + k, nt)))[phase]
            m = remote(
                (stats, stats_mid)[phase].at[which], stats_in.at[which, slot],
                stats_send.at[which, slot], stats_recv.at[which, slot], device,
            )
            m.start()
            stat_msgs[which, slot] = m

    def merged(which, phase):
        mine = (stats, stats_mid)[phase]
        slots = range(phase * (n - 1), phase * (n - 1) + (n, nt)[phase] - 1)
        for slot in slots:
            stat_msgs[which, slot].wait_recv()
        peaks = [mine[which, 0]] + [stats_in[which, slot, 0] for slot in slots]
        totals = [mine[which, 1]] + [stats_in[which, slot, 1] for slot in slots]
        top = functools.reduce(jnp.maximum, peaks)
        return top, sum(t * jnp.exp(p - top) for p, t in zip(peaks, totals))

    def stats_next(which):
        top, total = merged(which, 0)
        stats_mid[which, 0] = top
        stats_mid[which, 1] = total
        stats_out(which, 1)

    def stats_end(which):
        top, total = merged(which, 1)
        scale[which] = (2.0, 1.0)[which] * jnp.exp(stats[which, 0] - top) / total

    step_a(0)
    loads[0].wait()
    loads[1].wait()
    arrived(0, 12)
    held = logits(0, 0, 0, None)
    step_b(0)
    step_c(0)
    loads[2].wait()
    loads[3].wait()
    arrived(1, 12)
    logits(1, 0, 0, held)
    step_d(0)
    loads[4].wait()
    arrived(2, 12)
    held = logits(1, 0, 1, None)
    step_e(0)
    step_a(1)
    arrived(0, 13, 16)
    held = logits(0, 1, 0, held)
    step_b(1)
    arrived(0, 14, 17)
    held = logits(0, 2, 0, held)
    step_c(1)
    arrived(0, 15, 18)
    held = logits(0, 3, 0, held)
    rows_copy = pltpu.make_async_copy(s_rows, rows_out, out_sem.at[4])
    rows_copy.start()
    step_d(1)
    arrived(1, 13, 16)
    logits(1, 1, 0, held)
    stats_out(0, 0)
    step_e(1)
    step_a(2)
    arrived(1, 14, 17)
    logits(1, 2, 0, None)
    step_b(2)
    arrived(1, 15, 18)
    logits(1, 3, 0, None)
    step_c(2)
    stats_next(0)
    step_d(2)
    arrived(2, 13, 16)
    held = logits(1, 1, 1, None)
    step_e(2)
    arrived(2, 14, 17)
    held = logits(1, 2, 1, held)
    stats_end(0)
    arrived(2, 15, 18)
    held = logits(1, 3, 1, held)
    settle(held)
    for m in id_msgs:
        m.wait()

    def column_of(ref_row):
        return jnp.concatenate([as_column(ref_row(h)) for h in range(2)], axis=0)

    def student_part(d):
        rows = rows_of(d)
        s_scale = column_of(lambda h: scale[0, pl.ds(other(d) * 2 + h, 1), :])
        wanted = column_of(lambda h: ids[other(d) * 2 + h][:1, :])

        def step(j, carry):
            cols = cols_of(j)
            hit = jnp.where(wanted == column_ids(j).astype(jnp.float32), 1.0, 0.0)
            s_exp[rows, cols] = s_exp[rows, cols] * s_scale - hit
            return carry

        lax.fori_loop(0, tiles, step, 0)

    stats_out(1, 0)
    student_part(3)
    student_part(1)
    stats_next(1)
    student_part(2)
    student_part(0)
    stats_end(1)

    tokens = t_rows.shape[0]
    half = depth // 2
    grads = t_w
    outs, pairs, sent = [], {}, {}
    order = (3, 1, 2, 0)

    def teacher_scale(d):
        return column_of(lambda h: scale[1, pl.ds(other(d) * 2 + h, 1), :])

    def gradient(d, j, t_scale):
        rows, cols = rows_of(d), cols_of(j)
        g = s_exp[rows, cols] - t_exp[rows, cols] * t_scale
        grads[rows, cols] = g.astype(jnp.bfloat16)

    def back(d, following):
        rows = rows_of(d)
        t_scale = None if following is None else teacher_scale(following)

        def step(j, carry):
            cols = cols_of(j)
            t_exp[rows, cols] = lax.dot_general(
                grads[rows, :], s_w[cols, :], (((1,), (1,)), ((), ())), preferred_element_type=jnp.float32
            )
            if following is not None:
                gradient(following, j, t_scale)
            return carry

        lax.fori_loop(0, tiles, step, 0)
        theirs = pl.ds(pl.multiple_of(other(d) * pair + (1 - core) * block, block), block)
        pairs[d] = remote(t_exp.at[theirs], pair_in.at[d], pair_send.at[d], pair_recv.at[d], sibling)
        pairs[d].start()

    def grads_out(d):
        rows = rows_of(d)
        outs.append(pltpu.make_async_copy(grads.at[rows], grad_out.at[rows], out_sem.at[d]))
        outs[-1].start()

    def own_sum(d, h):
        mine = pl.ds(pl.multiple_of(other(d) * pair + core * block, block), block)
        cols = pl.ds(h * half, half)
        return t_exp[mine, cols] + pair_in[d, :, cols]

    def stage(d, h, value):
        place = grads.at[pl.ds(tokens + (d - 1) * block, block), pl.ds(h * half, half)]
        place[...] = value.astype(jnp.bfloat16)
        return place

    def hop(h):
        sent["hop", h] = remote(
            stage(3, h, own_sum(3, h)), hop_in.at[h], hop_send.at[h], hop_recv.at[h], near[h]
        )
        sent["hop", h].start()

    def plane(d, h, extra):
        value = own_sum(d, h)
        if extra:
            sent["hop", h].wait_recv()
            value = value + hop_in[h].astype(jnp.float32)
        sent[d, h] = remote(
            stage(d, h, value), plane_in.at[d - 1, h],
            plane_send.at[d - 1, h], plane_recv.at[d - 1, h], near[d - 1],
        )
        sent[d, h].start()

    t_scale = teacher_scale(3)

    def first_gradient(j, carry):
        gradient(3, j, t_scale)
        return carry

    lax.fori_loop(0, tiles, first_gradient, 0)
    grads_out(3)
    back(3, 1)
    grads_out(1)
    back(1, 2)
    pairs[3].wait()
    hop(0)
    hop(1)
    grads_out(2)
    back(2, 0)
    pairs[1].wait()
    plane(1, 0, False)
    grads_out(0)
    back(0, None)
    pairs[2].wait()
    plane(2, 1, False)
    plane(1, 1, True)
    plane(2, 0, True)
    pairs[0].wait()
    for h in range(2):
        s_exp[0:block, pl.ds(h * half, half)] = own_sum(0, h)
    for d, h in ((1, 0), (2, 1), (1, 1), (2, 0)):
        sent[d, h].wait_recv()
        s_exp[0:block, pl.ds(h * half, half)] += plane_in[d - 1, h].astype(jnp.float32)
    for k in range(nt):
        part = pl.ds(pl.multiple_of(lax.rem(tz + k, nt) * features, features), features)
        part_outs[k][...] = s_exp[0:block, part].astype(part_outs[k].dtype)
    for m in sent.values():
        m.wait_send()
    for m in stat_msgs.values():
        m.wait_send()
    for m in msgs.values():
        m.wait_send()
    for copy in outs:
        copy.wait()
    rows_copy.wait()


def head_kernel(rows_ref, grad_ref, out_ref):
    out_ref[...] = lax.dot_general(
        rows_ref[...], grad_ref[...], (((0,), (0,)), ((), ())), preferred_element_type=jnp.float32
    )


def head_gradient(student_rows, logit_grad):
    tokens, depth = student_rows.shape
    width = logit_grad.shape[1]
    strip = 256
    return pl.pallas_call(
        head_kernel,
        grid=(depth // strip,),
        in_specs=[
            pl.BlockSpec((tokens, strip), lambda i: (0, i)),
            pl.BlockSpec((tokens, width), lambda i: (0, 0)),
        ],
        out_specs=pl.BlockSpec((strip, width), lambda i: (i, 0)),
        out_shape=jax.ShapeDtypeStruct((depth, width), jnp.float32),
        compiler_params=pltpu.CompilerParams(vmem_limit_bytes=48 * 1024 * 1024),
        cost_estimate=pl.CostEstimate(
            flops=2 * tokens * depth * width,
            bytes_accessed=2 * tokens * (depth + width) + 4 * depth * width,
            transcendentals=0,
        ),
    )(student_rows, logit_grad)


def fused(n, nt, teacher_hidden, student_hidden, target_ids, teacher_head, student_head):
    block, teacher_depth = teacher_hidden.shape
    depth, width = student_head.shape
    tokens = n * block
    features = depth // nt
    half = depth // 2
    f32, bf16, dma = jnp.float32, jnp.bfloat16, pltpu.SemaphoreType.DMA
    anywhere = pl.BlockSpec(memory_space=pl.ANY)
    whole = pl.BlockSpec(memory_space=pltpu.VMEM)
    swaps = n - 1 + nt - 1
    logit_grad, student_rows, *parts = pl.pallas_call(
        functools.partial(kernel, n, nt, 1024 if width % 1024 == 0 else 512),
        out_shape=(
            jax.ShapeDtypeStruct((tokens, width), bf16),
            jax.ShapeDtypeStruct((tokens, depth), bf16),
            jax.ShapeDtypeStruct((block, features), f32),
        )
        + (jax.ShapeDtypeStruct((block, features), bf16),) * (nt - 1),
        in_specs=[anywhere, anywhere, whole, anywhere, anywhere],
        out_specs=(anywhere, anywhere) + (whole,) * nt,
        scratch_shapes=[
            pltpu.VMEM((tokens, teacher_depth), bf16),
            pltpu.VMEM((tokens, depth), bf16),
            pltpu.VMEM((n, 8, block), f32),
            pltpu.VMEM((teacher_depth, width), bf16),
            pltpu.VMEM((depth, width), bf16),
            pltpu.VMEM((tokens, width), f32),
            pltpu.VMEM((tokens, width), f32),
            pltpu.VMEM((2, 2, n, block), f32),
            pltpu.VMEM((2, swaps, 2, n, block), f32),
            pltpu.VMEM((2, 2, n, block), f32),
            pltpu.VMEM((2, n, block), f32),
            pltpu.VMEM((n // 2, block, depth), f32),
            pltpu.VMEM((2, block, half), bf16),
            pltpu.VMEM((2, 2, block, half), bf16),
            dma((5,)), dma((5,)),
            dma((PIECES, SLOTS)), dma((PIECES, SLOTS)),
            dma((n - 1,)), dma((n - 1,)),
            dma((2, swaps)), dma((2, swaps)),
            dma((n // 2,)), dma((n // 2,)),
            dma((2,)), dma((2,)),
            dma((2, 2)), dma((2, 2)),
        ],
        compiler_params=pltpu.CompilerParams(
            collective_id=0, has_side_effects=True, vmem_limit_bytes=67043328
        ),
    )(teacher_hidden, student_hidden, target_ids.reshape(1, block), teacher_head, student_head)
    input_grad = parts[0]
    arrived = []
    for k in range(1, nt):
        ring = [(i, (i + k) % nt) for i in range(nt)]
        arrived.append(lax.ppermute(parts[k], "tensor", ring))
    head_grad = head_gradient(student_rows, logit_grad)
    for other in arrived:
        input_grad = input_grad + other.astype(f32)
    return head_grad, input_grad


def choose(n, nt, *arrays):
    teacher_hidden, student_hidden, _, teacher_head, student_head = arrays
    block, width = teacher_hidden.shape[0], student_head.shape[1]
    fits = (
        n == 8
        and nt in (2, 4, 8)
        and block == 128
        and width == student_head.shape[0]
        and teacher_head.shape[0] % 256 == 0
        and width % 512 == 0
        and teacher_head.shape[0] >= n * block + 3 * block
    )
    return fused(n, nt, *arrays) if fits else body(*arrays)


def solution(mesh):
    placed = (
        P("dp", None),
        P("dp", None),
        P("dp"),
        P(None, ("dp", "tensor")),
        P(None, ("dp", "tensor")),
    )
    return jax.shard_map(
        functools.partial(choose, mesh.shape["dp"], mesh.shape["tensor"]),
        mesh=mesh,
        in_specs=placed,
        out_specs=(P(None, ("dp", "tensor")), P("dp", "tensor")),
        check_vma=False,
    )
```

```python
import functools

import jax
import jax.numpy as jnp
from jax import lax
from jax.experimental import pallas as pl
from jax.experimental.pallas import tpu as pltpu
from jax.sharding import PartitionSpec as P

VOCAB = 64128


def body(teacher_hidden, student_hidden, target_ids, teacher_head, student_head):
    width_cols = teacher_head.shape[1]
    first_col = (
        lax.axis_index("dp") * lax.axis_size("tensor") + lax.axis_index("tensor")
    ) * width_cols
    columns = first_col + lax.iota(jnp.int32, width_cols)
    is_real = (columns < VOCAB)[None, :]
    teacher_logits = jnp.dot(
        lax.all_gather(teacher_hidden, "dp", axis=0, tiled=True),
        teacher_head,
        preferred_element_type=jnp.float32,
    )
    teacher_logits = jnp.where(is_real, teacher_logits, jnp.float32(-1e30))
    student_rows, all_targets = (
        lax.all_gather(student_hidden, "dp", axis=0, tiled=True),
        lax.all_gather(target_ids, "dp", axis=0, tiled=True),
    )
    student_logits = jnp.where(
        is_real,
        jnp.dot(student_rows, student_head, preferred_element_type=jnp.float32),
        jnp.float32(-1e30),
    )
    peaks = jnp.stack([jnp.max(teacher_logits, axis=1), jnp.max(student_logits, axis=1)])
    totals = jnp.stack(
        [
            jnp.sum(jnp.exp(teacher_logits - peaks[0][:, None]), axis=1),
            jnp.sum(jnp.exp(student_logits - peaks[1][:, None]), axis=1),
        ]
    )
    table = lax.all_gather(jnp.concatenate([peaks, totals]), ("dp", "tensor"), axis=0)
    top = jnp.max(table[:, :2], axis=0)
    teacher_total, student_total = jnp.sum(table[:, 2:] * jnp.exp(table[:, :2] - top), axis=0)
    teacher_expo = jnp.exp(teacher_logits - top[0][:, None])
    student_expo = jnp.exp(student_logits - top[1][:, None])
    teacher_probs = teacher_expo / teacher_total[:, None]
    student_probs = student_expo / student_total[:, None]
    onehot = (all_targets[:, None] == columns[None, :]).astype(jnp.float32)
    logit_grad = (2.0 * student_probs - teacher_probs - onehot).astype(jnp.bfloat16)
    head_grad = lax.dot_general(
        student_rows, logit_grad, (((0,), (0,)), ((), ())), preferred_element_type=jnp.float32
    )
    own_rows = lax.psum_scatter(
        lax.dot_general(
            logit_grad, student_head, (((1,), (1,)), ((), ())), preferred_element_type=jnp.float32
        ),
        "dp",
        scatter_dimension=0,
        tiled=True,
    )
    input_grad = lax.psum_scatter(own_rows, "tensor", scatter_dimension=1, tiled=True)
    return (head_grad, input_grad)


MESH = pl.DeviceIdType.MESH
PIECES = 4
SLOTS = 19
PLAN = (
    (6, 0), (6, 0), (0, 0), (6, 1), (6, 1), (1, 0), (6, 2), (6, 2), (6, 3), (2, 0),
    (6, 3), (3, 0), (4, 0), (7, 0), (0, 1), (7, 0), (5, 0), (8, 0), (1, 1), (8, 0),
    (9, 0), (2, 1), (9, 0), (3, 1), (4, 1), (0, 2), (7, 1), (1, 2), (7, 1), (2, 2),
    (5, 1), (8, 1), (3, 2), (8, 1), (4, 2), (0, 3), (9, 1), (1, 3), (9, 1), (5, 2),
    (2, 3), (7, 2), (7, 2), (3, 3), (8, 2), (8, 2), (4, 3), (9, 2), (9, 2), (7, 3),
    (7, 3), (5, 3), (8, 3), (8, 3), (9, 3), (9, 3),
)


def as_column(row):
    return jnp.transpose(jnp.broadcast_to(row, (row.shape[1], row.shape[1])))[:, :1]


def as_row(column):
    return jnp.transpose(jnp.broadcast_to(column, (column.shape[0], column.shape[0])))[:1, :]


def kernel(
    n, nt, tile,
    teacher_in, student_in, ids_in, teacher_head, student_head,
    grad_out, rows_out, strip_out, *refs,
):
    part_outs = refs[:nt]
    (
        t_rows, s_rows, ids, t_w, s_w, t_exp, s_exp,
        stats, stats_in, stats_mid, scale, pair_in, hop_in, plane_in,
        local_sem, out_sem, strip_sem, gather_send, gather_recv, ids_send, ids_recv,
        stats_send, stats_recv, pair_send, pair_recv, hop_send, hop_recv, plane_send, plane_recv,
    ) = refs[nt:]
    block = teacher_in.shape[0]
    pair = 2 * block
    quarter = block // 4
    width = t_w.shape[1]
    depth = s_w.shape[0]
    slab = t_w.shape[0] // 2
    features = depth // nt
    dp = lax.axis_index("dp")
    tz = lax.axis_index("tensor")
    chip, core = dp // 2, dp % 2
    parity = tz % 2

    def flip(value, bit):
        return value + bit - 2 * bit * ((value // bit) % 2)

    def other(d):
        out = chip
        for bit in (1, 2):
            if d & bit:
                out = flip(out, bit)
        return out

    sibling = (chip * 2 + 1 - core, tz)
    near = ((other(1) * 2 + core, tz), (other(2) * 2 + core, tz))
    mate = (dp, flip(tz, 1))
    blocks = [other(d) * 2 + core for d in range(4)]
    own = pl.ds(pl.multiple_of(dp * block, block), block)

    loads = [
        pltpu.make_async_copy(student_head, s_w, local_sem.at[0]),
        pltpu.make_async_copy(student_in, s_rows.at[own], local_sem.at[1]),
        pltpu.make_async_copy(teacher_in, t_rows.at[own], local_sem.at[2]),
        pltpu.make_async_copy(teacher_head.at[0:slab], t_w.at[0:slab], local_sem.at[3]),
        pltpu.make_async_copy(teacher_head.at[slab:], t_w.at[slab:], local_sem.at[4]),
    ]
    for load in loads:
        load.start()
    ids[dp] = jnp.broadcast_to(ids_in[...].astype(jnp.float32), (8, block))

    barrier = pltpu.get_barrier_semaphore()
    for k in range(1, n):
        pl.semaphore_signal(barrier, inc=1, device_id=(lax.rem(dp + k, n), tz), device_id_type=MESH)
    for k in range(1, nt):
        pl.semaphore_signal(barrier, inc=1, device_id=(dp, lax.rem(tz + k, nt)), device_id_type=MESH)
    pl.semaphore_wait(barrier, n - 1 + nt - 1)

    def remote(source, target, send, recv, device):
        return pltpu.make_async_remote_copy(
            src_ref=source, dst_ref=target, send_sem=send, recv_sem=recv,
            device_id=device, device_id_type=MESH,
        )

    ends = (0, slab, slab + slab // 2, 2 * slab)
    pieces = ((student_in, s_rows, 0, depth),) + tuple(
        (teacher_in, t_rows, ends[i], ends[i + 1] - ends[i]) for i in range(3)
    )

    def at_quarter(i):
        return (i + parity * (3 - 2 * i)) * quarter

    first_half = parity * 2 * quarter
    second_half = (1 - parity) * 2 * quarter
    msgs = {}

    def send(p, slot):
        given, held, start, size = pieces[p]
        cols = pl.ds(start, size)
        x, y = near
        index, offset, count, device = {
            0: (0, at_quarter(0), quarter, x),
            1: (0, at_quarter(1), quarter, x),
            2: (2, at_quarter(0), quarter, x),
            3: (0, at_quarter(2), quarter, x),
            4: (0, at_quarter(0), quarter, y),
            5: (0, at_quarter(1), quarter, y),
            6: (1, at_quarter(1), quarter, y),
            7: (0, at_quarter(2), quarter, y),
            8: (1, at_quarter(0), quarter, mate),
            9: (2, at_quarter(0), quarter, mate),
            10: (3, at_quarter(0), quarter, mate),
            11: (3, at_quarter(1), quarter, mate),
            12: (0, 0, block, sibling),
            13: (1, first_half, 2 * quarter, sibling),
            14: (2, first_half, 2 * quarter, sibling),
            15: (3, first_half, 2 * quarter, sibling),
            16: (1, second_half, 2 * quarter, sibling),
            17: (2, second_half, 2 * quarter, sibling),
            18: (3, second_half, 2 * quarter, sibling),
        }[slot]
        target = pl.ds(pl.multiple_of(blocks[index] * block + offset, quarter), count)
        if index == 0:
            source = given.at[pl.ds(pl.multiple_of(offset, quarter), count), cols]
        else:
            source = held.at[target, cols]
        msgs[p, slot] = remote(
            source, held.at[target, cols], gather_send.at[p, slot], gather_recv.at[p, slot], device
        )
        msgs[p, slot].start()

    def arrived(p, *slots):
        for slot in slots:
            msgs[p, slot].wait_recv()

    for slot in (0, 4, 1, 5, 12):
        send(0, slot)
    for p in range(1, PIECES):
        send(p, 12)
    id_msgs = []
    for k in range(1, n):
        id_msgs.append(
            remote(ids.at[dp], ids.at[dp], ids_send.at[k - 1], ids_recv.at[k - 1], (lax.rem(dp + k, n), tz))
        )
        id_msgs[-1].start()

    def step_a(p):
        arrived(p, 4)
        send(p, 2)
        send(p, 9)
        arrived(p, 0)
        send(p, 8)
        send(p, 3)
        send(p, 7)

    def step_b(p):
        arrived(p, 1)
        send(p, 6)
        if p + 1 < PIECES:
            for slot in (0, 4, 1, 5):
                send(p + 1, slot)
        send(p, 13)
        arrived(p, 5)
        send(p, 14)

    def step_c(p):
        arrived(p, 2)
        send(p, 10)

    def step_d(p):
        arrived(p, 6)
        send(p, 11)
        send(p, 15)

    def step_f(p):
        arrived(p, 3, 8)
        send(p, 16)
        arrived(p, 7, 9)
        send(p, 17)

    def step_e(p):
        arrived(p, 10, 11)
        send(p, 18)

    first_col = (dp * nt + tz) * width
    tiles = width // tile

    def rows_of(d):
        return pl.ds(pl.multiple_of(other(d) * pair, pair), pair)

    def cols_of(j):
        return pl.ds(pl.multiple_of(j * tile, tile), tile)

    def column_ids(j):
        return first_col + j * tile + lax.broadcasted_iota(jnp.int32, (1, tile), 1)

    def exponential(held, cols):
        which, d, peak = held
        ref = (s_exp, t_exp)[which]
        e = jnp.exp(ref[rows_of(d), cols] - peak)
        ref[rows_of(d), cols] = e
        return jnp.sum(e, axis=1, keepdims=True)

    def record(held, total):
        which, d, peak = held
        for h in range(2):
            slot = pl.ds(other(d) * 2 + h, 1)
            stats[which, 0, slot, :] = as_row(peak[h * block : (h + 1) * block])
            stats[which, 1, slot, :] = as_row(total[h * block : (h + 1) * block])

    zero = jnp.zeros((pair, 1), jnp.float32)

    def logits(p, d, j, peak, total, held):
        _, rows_ref, start, size = pieces[p]
        which = min(p, 1)
        w_ref, z_ref = ((s_w, s_exp), (t_w, t_exp))[which]
        span = pl.ds(start, size)
        rows, cols = rows_of(d), pl.ds(j * tile, tile)
        z = jnp.dot(rows_ref[rows, span], w_ref[span, cols], preferred_element_type=jnp.float32)
        if start:
            z = z + z_ref[rows, cols]
        if start + size == rows_ref.shape[1]:
            z = jnp.where(column_ids(j) < VOCAB, z, jnp.float32(-1e30))
            peak = jnp.maximum(peak, jnp.max(z, axis=1, keepdims=True))
        z_ref[rows, cols] = z
        if held is not None:
            total = total + exponential(held, cols)
        return peak, total

    def settle(held):
        record(held, lax.fori_loop(0, tiles, lambda j, total: total + exponential(held, cols_of(j)), zero))

    stat_msgs = {}

    def stats_out(which, phase):
        for k in range(1, (n, nt)[phase]):
            slot = k - 1 + phase * (n - 1)
            device = ((lax.rem(dp + k, n), tz), (dp, lax.rem(tz + k, nt)))[phase]
            m = remote(
                (stats, stats_mid)[phase].at[which], stats_in.at[which, slot],
                stats_send.at[which, slot], stats_recv.at[which, slot], device,
            )
            m.start()
            stat_msgs[which, slot] = m

    def merged(which, phase):
        mine = (stats, stats_mid)[phase]
        slots = range(phase * (n - 1), phase * (n - 1) + (n, nt)[phase] - 1)
        for slot in slots:
            stat_msgs[which, slot].wait_recv()
        peaks = [mine[which, 0]] + [stats_in[which, slot, 0] for slot in slots]
        totals = [mine[which, 1]] + [stats_in[which, slot, 1] for slot in slots]
        top = functools.reduce(jnp.maximum, peaks)
        return top, sum(t * jnp.exp(p - top) for p, t in zip(peaks, totals))

    def stats_next(which):
        top, total = merged(which, 0)
        stats_mid[which, 0] = top
        stats_mid[which, 1] = total
        stats_out(which, 1)

    def stats_end(which):
        top, total = merged(which, 1)
        scale[which] = (2.0, 1.0)[which] * jnp.exp(stats[which, 0] - top) / total

    steps = (step_a, step_b, step_c, step_d, step_f, step_e)
    needs = ((12,), (13, 16), (14, 17), (15, 18))
    waits = ((0, 1), (2, 3), (4,), ())
    done, held, students = [], None, 0
    for kind, p in PLAN:
        if kind < len(steps):
            steps[kind](p)
            continue
        d = kind - len(steps)
        j = done.count((p, d))
        if j == 0:
            if d == 0:
                for i in waits[p]:
                    loads[i].wait()
            arrived(p, *needs[d])
            peak, total = zero - jnp.inf, zero
        peak, total = logits(p, d, j, peak, total, held)
        done.append((p, d))
        if j < tiles - 1:
            continue
        if held is not None:
            record(held, total)
            students += held[0] == 0
        held = (min(p, 1), d, peak) if p in (0, PIECES - 1) else None
        if students >= 4:
            if students == 4:
                rows_copy = pltpu.make_async_copy(s_rows, rows_out, out_sem.at[4])
                rows_copy.start()
                stats_out(0, 0)
            elif students == 6:
                stats_next(0)
            elif students == 8:
                stats_end(0)
            students += 1
    settle(held)
    for m in id_msgs:
        m.wait()

    def column_of(ref_row):
        return jnp.concatenate([as_column(ref_row(h)) for h in range(2)], axis=0)

    def student_part(d):
        rows = rows_of(d)
        s_scale = column_of(lambda h: scale[0, pl.ds(other(d) * 2 + h, 1), :])
        wanted = column_of(lambda h: ids[other(d) * 2 + h][:1, :])

        def step(j, carry):
            cols = cols_of(j)
            hit = jnp.where(wanted == column_ids(j).astype(jnp.float32), 1.0, 0.0)
            s_exp[rows, cols] = s_exp[rows, cols] * s_scale - hit
            return carry

        lax.fori_loop(0, tiles, step, 0)

    stats_out(1, 0)
    student_part(3)
    student_part(1)
    stats_next(1)
    student_part(2)
    student_part(0)
    stats_end(1)

    tokens = t_rows.shape[0]
    half = depth // 2
    grads = t_w
    outs, pairs, sent = [], {}, {}
    order = (3, 1, 2, 0)

    def teacher_scale(d):
        return column_of(lambda h: scale[1, pl.ds(other(d) * 2 + h, 1), :])

    def gradient(d, h, t_scale):
        rows, cols = rows_of(d), pl.ds(h * half, half)
        g = s_exp[rows, cols] - t_exp[rows, cols] * t_scale
        grads[rows, cols] = g.astype(jnp.bfloat16)

    def back(d, h, following=None, t_scale=None):
        rows, cols = rows_of(d), pl.ds(h * half, half)
        t_exp[rows, cols] = lax.dot_general(
            grads[rows, :], s_w[cols, :], (((1,), (1,)), ((), ())), preferred_element_type=jnp.float32
        )
        if following is not None:
            gradient(following, h, t_scale)
        theirs = pl.ds(pl.multiple_of(other(d) * pair + (1 - core) * block, block), block)
        pairs[d, h] = remote(
            t_exp.at[theirs, cols], pair_in.at[d, :, cols], pair_send.at[d, h], pair_recv.at[d, h], sibling
        )
        pairs[d, h].start()

    def grads_out(d):
        rows = rows_of(d)
        outs.append(pltpu.make_async_copy(grads.at[rows], grad_out.at[rows], out_sem.at[d]))
        outs[-1].start()

    def own_sum(d, h):
        pairs[d, h].wait_recv()
        mine = pl.ds(pl.multiple_of(other(d) * pair + core * block, block), block)
        cols = pl.ds(h * half, half)
        return t_exp[mine, cols] + pair_in[d, :, cols]

    def stage(d, h, value):
        place = grads.at[pl.ds(tokens + (d - 1) * block, block), pl.ds(h * half, half)]
        place[...] = value.astype(jnp.bfloat16)
        return place

    def hop(h):
        sent["hop", h] = remote(
            stage(3, h, own_sum(3, h)), hop_in.at[h], hop_send.at[h], hop_recv.at[h], near[h]
        )
        sent["hop", h].start()

    def plane(d, h, extra):
        value = own_sum(d, h)
        if extra:
            sent["hop", h].wait_recv()
            value = value + hop_in[h].astype(jnp.float32)
        sent[d, h] = remote(
            stage(d, h, value), plane_in.at[d - 1, h],
            plane_send.at[d - 1, h], plane_recv.at[d - 1, h], near[d - 1],
        )
        sent[d, h].start()

    t_scale = teacher_scale(3)
    gradient(3, 0, t_scale)
    gradient(3, 1, t_scale)
    grads_out(3)
    t_scale = teacher_scale(1)
    back(3, 0, 1, t_scale)
    back(3, 1, 1, t_scale)
    grads_out(1)
    t_scale = teacher_scale(2)
    back(1, 0, 2, t_scale)
    hop(0)
    back(1, 1, 2, t_scale)
    hop(1)
    grads_out(2)
    t_scale = teacher_scale(0)
    back(2, 0, 0, t_scale)
    plane(1, 0, False)
    back(2, 1, 0, t_scale)
    grads_out(0)
    back(0, 0)
    plane(2, 1, False)
    back(0, 1)
    plane(1, 1, True)
    plane(2, 0, True)
    lane, tall = strip_out.shape[1], depth // 4
    strips = []
    for i in range(4):
        place = s_exp.at[tokens // 2 : tokens // 2 + tall, i * lane : (i + 1) * lane]
        place[...] = lax.dot_general(
            s_rows[:, i * tall : (i + 1) * tall], grads[0:tokens, 0:lane],
            (((0,), (0,)), ((), ())), preferred_element_type=jnp.float32,
        )
        strips.append(
            pltpu.make_async_copy(place, strip_out.at[i * tall : (i + 1) * tall], strip_sem.at[i])
        )
        strips[-1].start()
    for h in range(2):
        s_exp[0:block, pl.ds(h * half, half)] = own_sum(0, h)
    for d, h in ((1, 0), (2, 1), (1, 1), (2, 0)):
        sent[d, h].wait_recv()
        s_exp[0:block, pl.ds(h * half, half)] += plane_in[d - 1, h].astype(jnp.float32)
    for k in range(nt):
        part = pl.ds(pl.multiple_of(lax.rem(tz + k, nt) * features, features), features)
        part_outs[k][...] = s_exp[0:block, part].astype(part_outs[k].dtype)
    for m in (*sent.values(), *pairs.values()):
        m.wait_send()
    for copy in strips:
        copy.wait()
    for m in stat_msgs.values():
        m.wait_send()
    for m in msgs.values():
        m.wait_send()
    for copy in outs:
        copy.wait()
    rows_copy.wait()


def head_kernel(
    rows_ref, grad_ref, strip_ref, out_ref, rows, grad, strip, tiles, rows_sem, grad_sem, out_sem, strip_sem
):
    lane, tall = strip_ref.shape[1], strip_ref.shape[0] // 4
    slots, _, wide = tiles.shape
    part = [slice(i * tall, (i + 1) * tall) for i in range(4)]
    strip_loads = [
        pltpu.make_async_copy(strip_ref.at[part[i]], strip.at[part[i]], strip_sem.at[i]) for i in range(4)
    ]
    strip_outs = [
        pltpu.make_async_copy(strip.at[part[i]], out_ref.at[part[i], 0:lane], strip_sem.at[4 + i])
        for i in range(4)
    ]
    row_loads = [
        pltpu.make_async_copy(
            rows_ref.at[:, i * tall : (i + 1) * tall], rows.at[:, i * tall : (i + 1) * tall], rows_sem.at[i]
        )
        for i in range(4)
    ]
    grad_loads = [
        pltpu.make_async_copy(
            grad_ref.at[:, lane + j * wide : lane + (j + 1) * wide],
            grad.at[:, j * wide : (j + 1) * wide],
            grad_sem.at[j],
        )
        for j in range(2)
    ]
    row_loads[0].start()
    for load in grad_loads + row_loads[1:] + strip_loads:
        load.start()
    outs = []
    for step in range(8):
        i, j = step // 2, step % 2
        if j == 0:
            row_loads[i].wait()
        if i == 0:
            grad_loads[j].wait()
        slot = step % slots
        if step >= slots:
            outs[step - slots].wait()
        tiles[slot] = lax.dot_general(
            rows[:, i * tall : (i + 1) * tall], grad[:, j * wide : (j + 1) * wide],
            (((0,), (0,)), ((), ())), preferred_element_type=jnp.float32,
        )
        outs.append(
            pltpu.make_async_copy(
                tiles.at[slot],
                out_ref.at[i * tall : (i + 1) * tall, lane + j * wide : lane + (j + 1) * wide],
                out_sem.at[slot],
            )
        )
        outs[-1].start()
        if 2 <= step < 6:
            strip_loads[step - 2].wait()
            strip_outs[step - 2].start()
    for copy in outs[-slots:] + strip_outs:
        copy.wait()


def head_gradient(student_rows, logit_grad, strip):
    tokens, depth = student_rows.shape
    width = logit_grad.shape[1]
    wide = (width - strip.shape[1]) // 2
    anywhere = pl.BlockSpec(memory_space=pl.ANY)
    dma = pltpu.SemaphoreType.DMA
    return pl.pallas_call(
        head_kernel,
        in_specs=[anywhere] * 3,
        out_specs=anywhere,
        out_shape=jax.ShapeDtypeStruct((depth, width), jnp.float32),
        scratch_shapes=[
            pltpu.VMEM((tokens, depth), jnp.bfloat16),
            pltpu.VMEM((tokens, 2 * wide), jnp.bfloat16),
            pltpu.VMEM(strip.shape, jnp.float32),
            pltpu.VMEM((4, depth // 4, wide), jnp.float32),
            dma((4,)), dma((2,)), dma((4,)), dma((8,)),
        ],
        compiler_params=pltpu.CompilerParams(vmem_limit_bytes=60 * 1024 * 1024),
        cost_estimate=pl.CostEstimate(
            flops=4 * tokens * depth * wide,
            bytes_accessed=2 * tokens * (depth + 2 * wide) + 4 * depth * (width + strip.shape[1]),
            transcendentals=0,
        ),
    )(student_rows, logit_grad, strip)


def fused(n, nt, teacher_hidden, student_hidden, target_ids, teacher_head, student_head):
    block, teacher_depth = teacher_hidden.shape
    depth, width = student_head.shape
    tokens = n * block
    features = depth // nt
    half = depth // 2
    f32, bf16, dma = jnp.float32, jnp.bfloat16, pltpu.SemaphoreType.DMA
    anywhere = pl.BlockSpec(memory_space=pl.ANY)
    whole = pl.BlockSpec(memory_space=pltpu.VMEM)
    swaps = n - 1 + nt - 1
    logit_grad, student_rows, strip, *parts = pl.pallas_call(
        functools.partial(kernel, n, nt, 1024),
        out_shape=(
            jax.ShapeDtypeStruct((tokens, width), bf16),
            jax.ShapeDtypeStruct((tokens, depth), bf16),
            jax.ShapeDtypeStruct((depth, width // 4), f32),
            jax.ShapeDtypeStruct((block, features), f32),
        )
        + (jax.ShapeDtypeStruct((block, features), bf16),) * (nt - 1),
        in_specs=[anywhere, anywhere, whole, anywhere, anywhere],
        out_specs=(anywhere,) * 3 + (whole,) * nt,
        scratch_shapes=[
            pltpu.VMEM((tokens, teacher_depth), bf16),
            pltpu.VMEM((tokens, depth), bf16),
            pltpu.VMEM((n, 8, block), f32),
            pltpu.VMEM((teacher_depth, width), bf16),
            pltpu.VMEM((depth, width), bf16),
            pltpu.VMEM((tokens, width), f32),
            pltpu.VMEM((tokens, width), f32),
            pltpu.VMEM((2, 2, n, block), f32),
            pltpu.VMEM((2, swaps, 2, n, block), f32),
            pltpu.VMEM((2, 2, n, block), f32),
            pltpu.VMEM((2, n, block), f32),
            pltpu.VMEM((n // 2, block, depth), f32),
            pltpu.VMEM((2, block, half), bf16),
            pltpu.VMEM((2, 2, block, half), bf16),
            dma((5,)), dma((5,)), dma((4,)),
            dma((PIECES, SLOTS)), dma((PIECES, SLOTS)),
            dma((n - 1,)), dma((n - 1,)),
            dma((2, swaps)), dma((2, swaps)),
            dma((n // 2, 2)), dma((n // 2, 2)),
            dma((2,)), dma((2,)),
            dma((2, 2)), dma((2, 2)),
        ],
        compiler_params=pltpu.CompilerParams(
            collective_id=0, has_side_effects=True, vmem_limit_bytes=67043328
        ),
    )(teacher_hidden, student_hidden, target_ids.reshape(1, block), teacher_head, student_head)
    input_grad = parts[0]
    arrived = []
    for k in range(1, nt):
        ring = [(i, (i + k) % nt) for i in range(nt)]
        arrived.append(lax.ppermute(parts[k], "tensor", ring))
    head_grad = head_gradient(student_rows, logit_grad, strip)
    for other in arrived:
        input_grad = input_grad + other.astype(f32)
    return head_grad, input_grad


def choose(n, nt, *arrays):
    teacher_hidden, student_hidden, _, teacher_head, student_head = arrays
    block, width = teacher_hidden.shape[0], student_head.shape[1]
    fits = (
        n == 8
        and nt in (2, 4, 8)
        and block == 128
        and width == student_head.shape[0]
        and teacher_head.shape[0] % 256 == 0
        and width % 1024 == 0
        and width <= 2 * n * block
        and teacher_head.shape[0] >= n * block + 3 * block
    )
    return fused(n, nt, *arrays) if fits else body(*arrays)


def solution(mesh):
    placed = (
        P("dp", None),
        P("dp", None),
        P("dp"),
        P(None, ("dp", "tensor")),
        P(None, ("dp", "tensor")),
    )
    return jax.shard_map(
        functools.partial(choose, mesh.shape["dp"], mesh.shape["tensor"]),
        mesh=mesh,
        in_specs=placed,
        out_specs=(P(None, ("dp", "tensor")), P("dp", "tensor")),
        check_vma=False,
    )
```

```python
import functools

import jax
import jax.numpy as jnp
from jax import lax
from jax.experimental import pallas as pl
from jax.experimental.pallas import tpu as pltpu
from jax.sharding import PartitionSpec as P

VOCAB = 64128


def body(teacher_hidden, student_hidden, target_ids, teacher_head, student_head):
    width_cols = teacher_head.shape[1]
    first_col = (
        lax.axis_index("dp") * lax.axis_size("tensor") + lax.axis_index("tensor")
    ) * width_cols
    columns = first_col + lax.iota(jnp.int32, width_cols)
    is_real = (columns < VOCAB)[None, :]
    teacher_logits = jnp.dot(
        lax.all_gather(teacher_hidden, "dp", axis=0, tiled=True),
        teacher_head,
        preferred_element_type=jnp.float32,
    )
    teacher_logits = jnp.where(is_real, teacher_logits, jnp.float32(-1e30))
    student_rows, all_targets = (
        lax.all_gather(student_hidden, "dp", axis=0, tiled=True),
        lax.all_gather(target_ids, "dp", axis=0, tiled=True),
    )
    student_logits = jnp.where(
        is_real,
        jnp.dot(student_rows, student_head, preferred_element_type=jnp.float32),
        jnp.float32(-1e30),
    )
    peaks = jnp.stack([jnp.max(teacher_logits, axis=1), jnp.max(student_logits, axis=1)])
    totals = jnp.stack(
        [
            jnp.sum(jnp.exp(teacher_logits - peaks[0][:, None]), axis=1),
            jnp.sum(jnp.exp(student_logits - peaks[1][:, None]), axis=1),
        ]
    )
    table = lax.all_gather(jnp.concatenate([peaks, totals]), ("dp", "tensor"), axis=0)
    top = jnp.max(table[:, :2], axis=0)
    teacher_total, student_total = jnp.sum(table[:, 2:] * jnp.exp(table[:, :2] - top), axis=0)
    teacher_expo = jnp.exp(teacher_logits - top[0][:, None])
    student_expo = jnp.exp(student_logits - top[1][:, None])
    teacher_probs = teacher_expo / teacher_total[:, None]
    student_probs = student_expo / student_total[:, None]
    onehot = (all_targets[:, None] == columns[None, :]).astype(jnp.float32)
    logit_grad = (2.0 * student_probs - teacher_probs - onehot).astype(jnp.bfloat16)
    head_grad = lax.dot_general(
        student_rows, logit_grad, (((0,), (0,)), ((), ())), preferred_element_type=jnp.float32
    )
    own_rows = lax.psum_scatter(
        lax.dot_general(
            logit_grad, student_head, (((1,), (1,)), ((), ())), preferred_element_type=jnp.float32
        ),
        "dp",
        scatter_dimension=0,
        tiled=True,
    )
    input_grad = lax.psum_scatter(own_rows, "tensor", scatter_dimension=1, tiled=True)
    return (head_grad, input_grad)


MESH = pl.DeviceIdType.MESH
PIECES = 4
SLOTS = 19
PLAN = (
    (6, 0), (6, 0), (0, 0), (6, 1), (6, 1), (1, 0), (6, 2), (6, 2), (6, 3), (2, 0),
    (6, 3), (4, 0), (3, 0), (7, 0), (0, 1), (7, 0), (8, 0), (5, 0), (1, 1), (8, 0),
    (9, 0), (2, 1), (9, 0), (4, 1), (3, 1), (0, 2), (7, 1), (1, 2), (7, 1), (2, 2),
    (8, 1), (5, 1), (3, 2), (8, 1), (0, 3), (9, 1), (4, 2), (1, 3), (9, 1), (2, 3),
    (7, 2), (5, 2), (7, 2), (3, 3), (8, 2), (8, 2), (9, 2), (4, 3), (9, 2), (7, 3),
    (7, 3), (5, 3), (8, 3), (8, 3), (9, 3), (9, 3),
)


def as_column(row):
    return jnp.transpose(jnp.broadcast_to(row, (row.shape[1], row.shape[1])))[:, :1]


def as_row(column):
    return jnp.transpose(jnp.broadcast_to(column, (column.shape[0], column.shape[0])))[:1, :]


def kernel(
    n, nt, tile,
    teacher_in, student_in, ids_in, teacher_head, student_head,
    grad_out, rows_out, *refs,
):
    part_outs = refs[:nt]
    (
        t_rows, s_rows, ids, t_w, s_w, t_exp, s_exp,
        stats, stats_in, stats_mid, scale, pair_in, hop_in, plane_in,
        local_sem, out_sem, gather_send, gather_recv, ids_send, ids_recv,
        stats_send, stats_recv, pair_send, pair_recv, hop_send, hop_recv, plane_send, plane_recv,
    ) = refs[nt:]
    block = teacher_in.shape[0]
    pair = 2 * block
    quarter = block // 4
    width = t_w.shape[1]
    depth = s_w.shape[0]
    slab = t_w.shape[0] // 2
    features = depth // nt
    dp = lax.axis_index("dp")
    tz = lax.axis_index("tensor")
    chip, core = dp // 2, dp % 2
    parity = tz % 2

    def flip(value, bit):
        return value + bit - 2 * bit * ((value // bit) % 2)

    def other(d):
        out = chip
        for bit in (1, 2):
            if d & bit:
                out = flip(out, bit)
        return out

    sibling = (chip * 2 + 1 - core, tz)
    near = ((other(1) * 2 + core, tz), (other(2) * 2 + core, tz))
    mate = (dp, flip(tz, 1))
    blocks = [other(d) * 2 + core for d in range(4)]
    own = pl.ds(pl.multiple_of(dp * block, block), block)

    loads = [
        pltpu.make_async_copy(student_head, s_w, local_sem.at[0]),
        pltpu.make_async_copy(student_in, s_rows.at[own], local_sem.at[1]),
        pltpu.make_async_copy(teacher_in, t_rows.at[own], local_sem.at[2]),
        pltpu.make_async_copy(teacher_head.at[0:slab], t_w.at[0:slab], local_sem.at[3]),
        pltpu.make_async_copy(teacher_head.at[slab:], t_w.at[slab:], local_sem.at[4]),
    ]
    for load in loads:
        load.start()
    ids[dp] = jnp.broadcast_to(ids_in[...].astype(jnp.float32), (8, block))

    barrier = pltpu.get_barrier_semaphore()
    for k in range(1, n):
        pl.semaphore_signal(barrier, inc=1, device_id=(lax.rem(dp + k, n), tz), device_id_type=MESH)
    for k in range(1, nt):
        pl.semaphore_signal(barrier, inc=1, device_id=(dp, lax.rem(tz + k, nt)), device_id_type=MESH)
    pl.semaphore_wait(barrier, n - 1 + nt - 1)

    def remote(source, target, send, recv, device):
        return pltpu.make_async_remote_copy(
            src_ref=source, dst_ref=target, send_sem=send, recv_sem=recv,
            device_id=device, device_id_type=MESH,
        )

    ends = (0, slab, slab + slab // 2, 2 * slab)
    pieces = ((student_in, s_rows, 0, depth),) + tuple(
        (teacher_in, t_rows, ends[i], ends[i + 1] - ends[i]) for i in range(3)
    )

    def at_quarter(i):
        return (i + parity * (3 - 2 * i)) * quarter

    first_half = parity * 2 * quarter
    second_half = (1 - parity) * 2 * quarter
    msgs = {}

    def send(p, slot):
        given, held, start, size = pieces[p]
        cols = pl.ds(start, size)
        x, y = near
        index, offset, count, device = {
            0: (0, at_quarter(0), quarter, x),
            1: (0, at_quarter(1), quarter, x),
            2: (2, at_quarter(0), quarter, x),
            3: (0, at_quarter(2), quarter, x),
            4: (0, at_quarter(0), quarter, y),
            5: (0, at_quarter(1), quarter, y),
            6: (1, at_quarter(1), quarter, y),
            7: (0, at_quarter(2), quarter, y),
            8: (1, at_quarter(0), quarter, mate),
            9: (2, at_quarter(0), quarter, mate),
            10: (3, at_quarter(0), quarter, mate),
            11: (3, at_quarter(1), quarter, mate),
            12: (0, 0, block, sibling),
            13: (1, first_half, 2 * quarter, sibling),
            14: (2, first_half, 2 * quarter, sibling),
            15: (3, first_half, 2 * quarter, sibling),
            16: (1, second_half, 2 * quarter, sibling),
            17: (2, second_half, 2 * quarter, sibling),
            18: (3, second_half, 2 * quarter, sibling),
        }[slot]
        target = pl.ds(pl.multiple_of(blocks[index] * block + offset, quarter), count)
        if index == 0:
            source = given.at[pl.ds(pl.multiple_of(offset, quarter), count), cols]
        else:
            source = held.at[target, cols]
        msgs[p, slot] = remote(
            source, held.at[target, cols], gather_send.at[p, slot], gather_recv.at[p, slot], device
        )
        msgs[p, slot].start()

    def arrived(p, *slots):
        for slot in slots:
            msgs[p, slot].wait_recv()

    for slot in (0, 4, 1, 5, 12):
        send(0, slot)
    for p in range(1, PIECES):
        send(p, 12)
    id_msgs = []
    for k in range(1, n):
        id_msgs.append(
            remote(ids.at[dp], ids.at[dp], ids_send.at[k - 1], ids_recv.at[k - 1], (lax.rem(dp + k, n), tz))
        )
        id_msgs[-1].start()

    def step_a(p):
        arrived(p, 4)
        send(p, 2)
        send(p, 9)
        arrived(p, 0)
        send(p, 8)
        send(p, 3)
        send(p, 7)

    def step_b(p):
        arrived(p, 1)
        send(p, 6)
        if p + 1 < PIECES:
            for slot in (0, 4, 1, 5):
                send(p + 1, slot)
        send(p, 13)
        arrived(p, 5)
        send(p, 14)

    def step_c(p):
        arrived(p, 2)
        send(p, 10)

    def step_d(p):
        arrived(p, 6)
        send(p, 11)
        send(p, 15)

    def step_f(p):
        arrived(p, 3, 8)
        send(p, 16)
        arrived(p, 7, 9)
        send(p, 17)

    def step_e(p):
        arrived(p, 10, 11)
        send(p, 18)

    first_col = (dp * nt + tz) * width
    tiles = width // tile

    def rows_of(d):
        return pl.ds(pl.multiple_of(other(d) * pair, pair), pair)

    def cols_of(j):
        return pl.ds(pl.multiple_of(j * tile, tile), tile)

    def column_ids(j):
        return first_col + j * tile + lax.broadcasted_iota(jnp.int32, (1, tile), 1)

    def exponential(held, cols):
        which, d, peak = held
        ref = (s_exp, t_exp)[which]
        e = jnp.exp(ref[rows_of(d), cols] - peak)
        ref[rows_of(d), cols] = e
        return jnp.sum(e, axis=1, keepdims=True)

    def record(held, total):
        which, d, peak = held
        for h in range(2):
            slot = pl.ds(other(d) * 2 + h, 1)
            stats[which, 0, slot, :] = as_row(peak[h * block : (h + 1) * block])
            stats[which, 1, slot, :] = as_row(total[h * block : (h + 1) * block])

    zero = jnp.zeros((pair, 1), jnp.float32)

    def logits(p, d, j, peak, total, held):
        _, rows_ref, start, size = pieces[p]
        which = min(p, 1)
        w_ref, z_ref = ((s_w, s_exp), (t_w, t_exp))[which]
        span = pl.ds(start, size)
        last = start + size == rows_ref.shape[1]
        rows, cols = rows_of(d), pl.ds(j * tile, tile)
        z = jnp.dot(rows_ref[rows, span], w_ref[span, cols], preferred_element_type=jnp.float32)
        if start:
            z = z + z_ref[rows, cols]
        if last:
            z = jnp.where(column_ids(j) < VOCAB, z, jnp.float32(-1e30))
            peak = jnp.maximum(peak, jnp.max(z, axis=1, keepdims=True))
        z_ref[rows, cols] = z
        if held is not None:
            total = total + exponential(held, cols)
        return peak, total

    def settle(held):
        record(held, lax.fori_loop(0, tiles, lambda j, total: total + exponential(held, cols_of(j)), zero))

    stat_msgs = {}

    def stats_out(which, phase):
        for k in range(1, (n, nt)[phase]):
            slot = k - 1 + phase * (n - 1)
            device = ((lax.rem(dp + k, n), tz), (dp, lax.rem(tz + k, nt)))[phase]
            m = remote(
                (stats, stats_mid)[phase].at[which], stats_in.at[which, slot],
                stats_send.at[which, slot], stats_recv.at[which, slot], device,
            )
            m.start()
            stat_msgs[which, slot] = m

    def merged(which, phase):
        mine = (stats, stats_mid)[phase]
        slots = range(phase * (n - 1), phase * (n - 1) + (n, nt)[phase] - 1)
        for slot in slots:
            stat_msgs[which, slot].wait_recv()
        peaks = [mine[which, 0]] + [stats_in[which, slot, 0] for slot in slots]
        totals = [mine[which, 1]] + [stats_in[which, slot, 1] for slot in slots]
        top = functools.reduce(jnp.maximum, peaks)
        return top, sum(t * jnp.exp(p - top) for p, t in zip(peaks, totals))

    def stats_next(which):
        top, total = merged(which, 0)
        stats_mid[which, 0] = top
        stats_mid[which, 1] = total
        stats_out(which, 1)

    def stats_end(which):
        top, total = merged(which, 1)
        scale[which] = (2.0, 1.0)[which] * jnp.exp(stats[which, 0] - top) / total

    steps = (step_a, step_b, step_c, step_d, step_f, step_e)
    needs = ((12,), (13, 16), (14, 17), (15, 18))
    waits = ((0, 1), (2, 3), (4,), ())
    done, held, students = [], None, 0
    for kind, p in PLAN:
        if kind < len(steps):
            steps[kind](p)
            continue
        d = kind - len(steps)
        j = done.count((p, d))
        if j == 0:
            if d == 0:
                for i in waits[p]:
                    loads[i].wait()
            arrived(p, *needs[d])
            peak, total = zero - jnp.inf, zero
        peak, total = logits(p, d, j, peak, total, held)
        done.append((p, d))
        if j < tiles - 1:
            continue
        if held is not None:
            record(held, total)
            students += held[0] == 0
        held = (min(p, 1), d, peak) if p in (0, PIECES - 1) else None
        if students >= 4:
            if students == 4:
                rows_copy = pltpu.make_async_copy(s_rows, rows_out, out_sem.at[4])
                rows_copy.start()
                stats_out(0, 0)
            elif students == 6:
                stats_next(0)
            elif students == 8:
                stats_end(0)
            students += 1
    settle(held)
    for m in id_msgs:
        m.wait()

    def column_of(ref_row):
        return jnp.concatenate([as_column(ref_row(h)) for h in range(2)], axis=0)

    def student_part(d):
        rows = rows_of(d)
        s_scale = column_of(lambda h: scale[0, pl.ds(other(d) * 2 + h, 1), :])
        wanted = column_of(lambda h: ids[other(d) * 2 + h][:1, :])

        def step(j, carry):
            cols = cols_of(j)
            hit = jnp.where(wanted == column_ids(j).astype(jnp.float32), 1.0, 0.0)
            s_exp[rows, cols] = s_exp[rows, cols] * s_scale - hit
            return carry

        lax.fori_loop(0, tiles, step, 0)

    stats_out(1, 0)
    student_part(3)
    student_part(1)
    stats_next(1)
    student_part(2)
    student_part(0)
    stats_end(1)

    tokens = t_rows.shape[0]
    half = depth // 2
    grads = t_w
    outs, pairs, sent = [], {}, {}
    order = (3, 1, 2, 0)

    def teacher_scale(d):
        return column_of(lambda h: scale[1, pl.ds(other(d) * 2 + h, 1), :])

    def gradient(d, j, t_scale):
        rows, cols = rows_of(d), cols_of(j)
        g = s_exp[rows, cols] - t_exp[rows, cols] * t_scale
        grads[rows, cols] = g.astype(jnp.bfloat16)

    def back(d, following):
        rows = rows_of(d)
        t_scale = None if following is None else teacher_scale(following)

        def step(j, carry):
            cols = cols_of(j)
            t_exp[rows, cols] = lax.dot_general(
                grads[rows, :], s_w[cols, :], (((1,), (1,)), ((), ())), preferred_element_type=jnp.float32
            )
            if following is not None:
                gradient(following, j, t_scale)
            return carry

        lax.fori_loop(0, tiles, step, 0)
        theirs = pl.ds(pl.multiple_of(other(d) * pair + (1 - core) * block, block), block)
        pairs[d] = remote(t_exp.at[theirs], pair_in.at[d], pair_send.at[d], pair_recv.at[d], sibling)
        pairs[d].start()

    def grads_out(d):
        rows = rows_of(d)
        outs.append(pltpu.make_async_copy(grads.at[rows], grad_out.at[rows], out_sem.at[d]))
        outs[-1].start()

    def own_sum(d, h):
        mine = pl.ds(pl.multiple_of(other(d) * pair + core * block, block), block)
        cols = pl.ds(h * half, half)
        return t_exp[mine, cols] + pair_in[d, :, cols]

    def stage(d, h, value):
        place = grads.at[pl.ds(tokens + (d - 1) * block, block), pl.ds(h * half, half)]
        place[...] = value.astype(jnp.bfloat16)
        return place

    def hop(h):
        sent["hop", h] = remote(
            stage(3, h, own_sum(3, h)), hop_in.at[h], hop_send.at[h], hop_recv.at[h], near[h]
        )
        sent["hop", h].start()

    def plane(d, h, extra):
        value = own_sum(d, h)
        if extra:
            sent["hop", h].wait_recv()
            value = value + hop_in[h].astype(jnp.float32)
        sent[d, h] = remote(
            stage(d, h, value), plane_in.at[d - 1, h],
            plane_send.at[d - 1, h], plane_recv.at[d - 1, h], near[d - 1],
        )
        sent[d, h].start()

    t_scale = teacher_scale(3)

    def first_gradient(j, carry):
        gradient(3, j, t_scale)
        return carry

    lax.fori_loop(0, tiles, first_gradient, 0)
    grads_out(3)
    back(3, 1)
    grads_out(1)
    back(1, 2)
    pairs[3].wait()
    hop(0)
    hop(1)
    grads_out(2)
    back(2, 0)
    pairs[1].wait()
    plane(1, 0, False)
    grads_out(0)
    back(0, None)
    pairs[2].wait()
    plane(2, 1, False)
    plane(1, 1, True)
    plane(2, 0, True)
    pairs[0].wait()
    for h in range(2):
        s_exp[0:block, pl.ds(h * half, half)] = own_sum(0, h)
    for d, h in ((1, 0), (2, 1), (1, 1), (2, 0)):
        sent[d, h].wait_recv()
        s_exp[0:block, pl.ds(h * half, half)] += plane_in[d - 1, h].astype(jnp.float32)
    for k in range(nt):
        part = pl.ds(pl.multiple_of(lax.rem(tz + k, nt) * features, features), features)
        part_outs[k][...] = s_exp[0:block, part].astype(part_outs[k].dtype)
    for m in sent.values():
        m.wait_send()
    for m in stat_msgs.values():
        m.wait_send()
    for m in msgs.values():
        m.wait_send()
    for copy in outs:
        copy.wait()
    rows_copy.wait()


def head_kernel(rows_ref, grad_ref, out_ref):
    out_ref[...] = lax.dot_general(
        rows_ref[...], grad_ref[...], (((0,), (0,)), ((), ())), preferred_element_type=jnp.float32
    )


def head_gradient(student_rows, logit_grad):
    tokens, depth = student_rows.shape
    width = logit_grad.shape[1]
    strip = 256
    return pl.pallas_call(
        head_kernel,
        grid=(depth // strip,),
        in_specs=[
            pl.BlockSpec((tokens, strip), lambda i: (0, i)),
            pl.BlockSpec((tokens, width), lambda i: (0, 0)),
        ],
        out_specs=pl.BlockSpec((strip, width), lambda i: (i, 0)),
        out_shape=jax.ShapeDtypeStruct((depth, width), jnp.float32),
        compiler_params=pltpu.CompilerParams(vmem_limit_bytes=62 * 1024 * 1024),
        cost_estimate=pl.CostEstimate(
            flops=2 * tokens * depth * width,
            bytes_accessed=2 * tokens * (depth + width) + 4 * depth * width,
            transcendentals=0,
        ),
    )(student_rows, logit_grad)


def fused(n, nt, teacher_hidden, student_hidden, target_ids, teacher_head, student_head):
    block, teacher_depth = teacher_hidden.shape
    depth, width = student_head.shape
    tokens = n * block
    features = depth // nt
    half = depth // 2
    f32, bf16, dma = jnp.float32, jnp.bfloat16, pltpu.SemaphoreType.DMA
    anywhere = pl.BlockSpec(memory_space=pl.ANY)
    whole = pl.BlockSpec(memory_space=pltpu.VMEM)
    swaps = n - 1 + nt - 1
    logit_grad, student_rows, *parts = pl.pallas_call(
        functools.partial(kernel, n, nt, width // 2),
        out_shape=(
            jax.ShapeDtypeStruct((tokens, width), bf16),
            jax.ShapeDtypeStruct((tokens, depth), bf16),
            jax.ShapeDtypeStruct((block, features), f32),
        )
        + (jax.ShapeDtypeStruct((block, features), bf16),) * (nt - 1),
        in_specs=[anywhere, anywhere, whole, anywhere, anywhere],
        out_specs=(anywhere, anywhere) + (whole,) * nt,
        scratch_shapes=[
            pltpu.VMEM((tokens, teacher_depth), bf16),
            pltpu.VMEM((tokens, depth), bf16),
            pltpu.VMEM((n, 8, block), f32),
            pltpu.VMEM((teacher_depth, width), bf16),
            pltpu.VMEM((depth, width), bf16),
            pltpu.VMEM((tokens, width), f32),
            pltpu.VMEM((tokens, width), f32),
            pltpu.VMEM((2, 2, n, block), f32),
            pltpu.VMEM((2, swaps, 2, n, block), f32),
            pltpu.VMEM((2, 2, n, block), f32),
            pltpu.VMEM((2, n, block), f32),
            pltpu.VMEM((n // 2, block, depth), f32),
            pltpu.VMEM((2, block, half), bf16),
            pltpu.VMEM((2, 2, block, half), bf16),
            dma((5,)), dma((5,)),
            dma((PIECES, SLOTS)), dma((PIECES, SLOTS)),
            dma((n - 1,)), dma((n - 1,)),
            dma((2, swaps)), dma((2, swaps)),
            dma((n // 2,)), dma((n // 2,)),
            dma((2,)), dma((2,)),
            dma((2, 2)), dma((2, 2)),
        ],
        compiler_params=pltpu.CompilerParams(
            collective_id=0, has_side_effects=True, vmem_limit_bytes=67043328
        ),
    )(teacher_hidden, student_hidden, target_ids.reshape(1, block), teacher_head, student_head)
    input_grad = parts[0]
    arrived = []
    for k in range(1, nt):
        ring = [(i, (i + k) % nt) for i in range(nt)]
        arrived.append(lax.ppermute(parts[k], "tensor", ring))
    head_grad = head_gradient(student_rows, logit_grad)
    for other in arrived:
        input_grad = input_grad + other.astype(f32)
    return head_grad, input_grad


def choose(n, nt, *arrays):
    teacher_hidden, student_hidden, _, teacher_head, student_head = arrays
    block, width = teacher_hidden.shape[0], student_head.shape[1]
    fits = (
        n == 8
        and nt in (2, 4, 8)
        and block == 128
        and width == student_head.shape[0]
        and teacher_head.shape[0] % 512 == 0
        and width % 512 == 0
        and teacher_head.shape[0] >= n * block + 3 * block
    )
    return fused(n, nt, *arrays) if fits else body(*arrays)


def solution(mesh):
    placed = (
        P("dp", None),
        P("dp", None),
        P("dp"),
        P(None, ("dp", "tensor")),
        P(None, ("dp", "tensor")),
    )
    return jax.shard_map(
        functools.partial(choose, mesh.shape["dp"], mesh.shape["tensor"]),
        mesh=mesh,
        in_specs=placed,
        out_specs=(P(None, ("dp", "tensor")), P("dp", "tensor")),
        check_vma=False,
    )
```

```python
import functools

import jax
import jax.numpy as jnp
from jax import lax
from jax.experimental import pallas as pl
from jax.experimental.pallas import tpu as pltpu
from jax.sharding import PartitionSpec as P

VOCAB = 64128


def body(teacher_hidden, student_hidden, target_ids, teacher_head, student_head):
    width_cols = teacher_head.shape[1]
    first_col = (
        lax.axis_index("dp") * lax.axis_size("tensor") + lax.axis_index("tensor")
    ) * width_cols
    columns = first_col + lax.iota(jnp.int32, width_cols)
    is_real = (columns < VOCAB)[None, :]
    teacher_logits = jnp.dot(
        lax.all_gather(teacher_hidden, "dp", axis=0, tiled=True),
        teacher_head,
        preferred_element_type=jnp.float32,
    )
    teacher_logits = jnp.where(is_real, teacher_logits, jnp.float32(-1e30))
    student_rows, all_targets = (
        lax.all_gather(student_hidden, "dp", axis=0, tiled=True),
        lax.all_gather(target_ids, "dp", axis=0, tiled=True),
    )
    student_logits = jnp.where(
        is_real,
        jnp.dot(student_rows, student_head, preferred_element_type=jnp.float32),
        jnp.float32(-1e30),
    )
    peaks = jnp.stack([jnp.max(teacher_logits, axis=1), jnp.max(student_logits, axis=1)])
    totals = jnp.stack(
        [
            jnp.sum(jnp.exp(teacher_logits - peaks[0][:, None]), axis=1),
            jnp.sum(jnp.exp(student_logits - peaks[1][:, None]), axis=1),
        ]
    )
    table = lax.all_gather(jnp.concatenate([peaks, totals]), ("dp", "tensor"), axis=0)
    top = jnp.max(table[:, :2], axis=0)
    teacher_total, student_total = jnp.sum(table[:, 2:] * jnp.exp(table[:, :2] - top), axis=0)
    teacher_expo = jnp.exp(teacher_logits - top[0][:, None])
    student_expo = jnp.exp(student_logits - top[1][:, None])
    teacher_probs = teacher_expo / teacher_total[:, None]
    student_probs = student_expo / student_total[:, None]
    onehot = (all_targets[:, None] == columns[None, :]).astype(jnp.float32)
    logit_grad = (2.0 * student_probs - teacher_probs - onehot).astype(jnp.bfloat16)
    head_grad = lax.dot_general(
        student_rows, logit_grad, (((0,), (0,)), ((), ())), preferred_element_type=jnp.float32
    )
    own_rows = lax.psum_scatter(
        lax.dot_general(
            logit_grad, student_head, (((1,), (1,)), ((), ())), preferred_element_type=jnp.float32
        ),
        "dp",
        scatter_dimension=0,
        tiled=True,
    )
    input_grad = lax.psum_scatter(own_rows, "tensor", scatter_dimension=1, tiled=True)
    return (head_grad, input_grad)


MESH = pl.DeviceIdType.MESH
PIECES = 4
SLOTS = 19
PLAN = (
    (6, 0), (6, 0), (0, 0), (6, 1), (6, 1), (1, 0), (6, 2), (6, 2), (6, 3), (2, 0),
    (6, 3), (4, 0), (3, 0), (7, 0), (0, 1), (7, 0), (8, 0), (5, 0), (1, 1), (8, 0),
    (9, 0), (2, 1), (9, 0), (4, 1), (3, 1), (0, 2), (7, 1), (1, 2), (7, 1), (2, 2),
    (8, 1), (5, 1), (3, 2), (8, 1), (0, 3), (9, 1), (4, 2), (1, 3), (9, 1), (2, 3),
    (7, 2), (5, 2), (7, 2), (3, 3), (8, 2), (8, 2), (9, 2), (4, 3), (9, 2), (7, 3),
    (7, 3), (5, 3), (8, 3), (8, 3), (9, 3), (9, 3),
)


def as_column(row):
    return jnp.transpose(jnp.broadcast_to(row, (row.shape[1], row.shape[1])))[:, :1]


def as_row(column):
    return jnp.transpose(jnp.broadcast_to(column, (column.shape[0], column.shape[0])))[:1, :]


def kernel(
    n, nt, tile,
    teacher_in, student_in, ids_in, teacher_head, student_head,
    grad_out, rows_out, *refs,
):
    part_outs = refs[:nt]
    (
        t_rows, s_rows, ids, t_w, s_w, t_exp, s_exp,
        stats, stats_in, stats_mid, scale, pair_in, hop_in, plane_in,
        local_sem, out_sem, gather_send, gather_recv, ids_send, ids_recv,
        stats_send, stats_recv, pair_send, pair_recv, hop_send, hop_recv, plane_send, plane_recv,
    ) = refs[nt:]
    block = teacher_in.shape[0]
    pair = 2 * block
    quarter = block // 4
    width = t_w.shape[1]
    depth = s_w.shape[0]
    slab = t_w.shape[0] // 2
    features = depth // nt
    dp = lax.axis_index("dp")
    tz = lax.axis_index("tensor")
    chip, core = dp // 2, dp % 2
    parity = tz % 2

    def flip(value, bit):
        return value + bit - 2 * bit * ((value // bit) % 2)

    def other(d):
        out = chip
        for bit in (1, 2):
            if d & bit:
                out = flip(out, bit)
        return out

    sibling = (chip * 2 + 1 - core, tz)
    near = ((other(1) * 2 + core, tz), (other(2) * 2 + core, tz))
    mate = (dp, flip(tz, 1))
    blocks = [other(d) * 2 + core for d in range(4)]
    own = pl.ds(pl.multiple_of(dp * block, block), block)

    loads = [
        pltpu.make_async_copy(student_head, s_w, local_sem.at[0]),
        pltpu.make_async_copy(student_in, s_rows.at[own], local_sem.at[1]),
        pltpu.make_async_copy(teacher_in, t_rows.at[own], local_sem.at[2]),
        pltpu.make_async_copy(teacher_head.at[0:slab], t_w.at[0:slab], local_sem.at[3]),
        pltpu.make_async_copy(teacher_head.at[slab:], t_w.at[slab:], local_sem.at[4]),
    ]
    for load in loads:
        load.start()
    ids[dp] = jnp.broadcast_to(ids_in[...].astype(jnp.float32), (8, block))

    barrier = pltpu.get_barrier_semaphore()
    for k in range(1, n):
        pl.semaphore_signal(barrier, inc=1, device_id=(lax.rem(dp + k, n), tz), device_id_type=MESH)
    for k in range(1, nt):
        pl.semaphore_signal(barrier, inc=1, device_id=(dp, lax.rem(tz + k, nt)), device_id_type=MESH)
    pl.semaphore_wait(barrier, n - 1 + nt - 1)

    def remote(source, target, send, recv, device):
        return pltpu.make_async_remote_copy(
            src_ref=source, dst_ref=target, send_sem=send, recv_sem=recv,
            device_id=device, device_id_type=MESH,
        )

    ends = (0, slab, slab + slab // 2, 2 * slab)
    pieces = ((student_in, s_rows, 0, depth),) + tuple(
        (teacher_in, t_rows, ends[i], ends[i + 1] - ends[i]) for i in range(3)
    )

    def at_quarter(i):
        return (i + parity * (3 - 2 * i)) * quarter

    first_half = parity * 2 * quarter
    second_half = (1 - parity) * 2 * quarter
    msgs = {}

    def send(p, slot):
        given, held, start, size = pieces[p]
        cols = pl.ds(start, size)
        x, y = near
        index, offset, count, device = {
            0: (0, at_quarter(0), quarter, x),
            1: (0, at_quarter(1), quarter, x),
            2: (2, at_quarter(0), quarter, x),
            3: (0, at_quarter(2), quarter, x),
            4: (0, at_quarter(0), quarter, y),
            5: (0, at_quarter(1), quarter, y),
            6: (1, at_quarter(1), quarter, y),
            7: (0, at_quarter(2), quarter, y),
            8: (1, at_quarter(0), quarter, mate),
            9: (2, at_quarter(0), quarter, mate),
            10: (3, at_quarter(0), quarter, mate),
            11: (3, at_quarter(1), quarter, mate),
            12: (0, 0, block, sibling),
            13: (1, first_half, 2 * quarter, sibling),
            14: (2, first_half, 2 * quarter, sibling),
            15: (3, first_half, 2 * quarter, sibling),
            16: (1, second_half, 2 * quarter, sibling),
            17: (2, second_half, 2 * quarter, sibling),
            18: (3, second_half, 2 * quarter, sibling),
        }[slot]
        target = pl.ds(pl.multiple_of(blocks[index] * block + offset, quarter), count)
        if index == 0:
            source = given.at[pl.ds(pl.multiple_of(offset, quarter), count), cols]
        else:
            source = held.at[target, cols]
        msgs[p, slot] = remote(
            source, held.at[target, cols], gather_send.at[p, slot], gather_recv.at[p, slot], device
        )
        msgs[p, slot].start()

    def arrived(p, *slots):
        for slot in slots:
            msgs[p, slot].wait_recv()

    for slot in (0, 4, 1, 5, 12):
        send(0, slot)
    for p in range(1, PIECES):
        send(p, 12)
    id_msgs = []
    for k in range(1, n):
        id_msgs.append(
            remote(ids.at[dp], ids.at[dp], ids_send.at[k - 1], ids_recv.at[k - 1], (lax.rem(dp + k, n), tz))
        )
        id_msgs[-1].start()

    def step_a(p):
        arrived(p, 4)
        send(p, 2)
        send(p, 9)
        arrived(p, 0)
        send(p, 8)
        send(p, 3)
        send(p, 7)

    def step_b(p):
        arrived(p, 1)
        send(p, 6)
        if p + 1 < PIECES:
            for slot in (0, 4, 1, 5):
                send(p + 1, slot)
        send(p, 13)
        arrived(p, 5)
        send(p, 14)

    def step_c(p):
        arrived(p, 2)
        send(p, 10)

    def step_d(p):
        arrived(p, 6)
        send(p, 11)
        send(p, 15)

    def step_f(p):
        arrived(p, 3, 8)
        send(p, 16)
        arrived(p, 7, 9)
        send(p, 17)

    def step_e(p):
        arrived(p, 10, 11)
        send(p, 18)

    first_col = (dp * nt + tz) * width
    tiles = width // tile

    def rows_of(d):
        return pl.ds(pl.multiple_of(other(d) * pair, pair), pair)

    def cols_of(j):
        return pl.ds(pl.multiple_of(j * tile, tile), tile)

    def column_ids(j):
        return first_col + j * tile + lax.broadcasted_iota(jnp.int32, (1, tile), 1)

    def exponential(held, cols):
        which, d, peak = held
        ref = (s_exp, t_exp)[which]
        e = jnp.exp(ref[rows_of(d), cols] - peak)
        ref[rows_of(d), cols] = e
        return jnp.sum(e, axis=1, keepdims=True)

    def record(held, total):
        which, d, peak = held
        for h in range(2):
            slot = pl.ds(other(d) * 2 + h, 1)
            stats[which, 0, slot, :] = as_row(peak[h * block : (h + 1) * block])
            stats[which, 1, slot, :] = as_row(total[h * block : (h + 1) * block])

    zero = jnp.zeros((pair, 1), jnp.float32)

    def logits(p, d, j, peak, total, held):
        _, rows_ref, start, size = pieces[p]
        which = min(p, 1)
        w_ref, z_ref = ((s_w, s_exp), (t_w, t_exp))[which]
        span = pl.ds(start, size)
        last = start + size == rows_ref.shape[1]
        rows, cols = rows_of(d), pl.ds(j * tile, tile)
        z = jnp.dot(rows_ref[rows, span], w_ref[span, cols], preferred_element_type=jnp.float32)
        if start:
            z = z + z_ref[rows, cols]
        if last:
            z = jnp.where(column_ids(j) < VOCAB, z, jnp.float32(-1e30))
            peak = jnp.maximum(peak, jnp.max(z, axis=1, keepdims=True))
        z_ref[rows, cols] = z
        if held is not None:
            total = total + exponential(held, cols)
        return peak, total

    def settle(held):
        record(held, lax.fori_loop(0, tiles, lambda j, total: total + exponential(held, cols_of(j)), zero))

    stat_msgs = {}

    def stats_out(which, phase):
        for k in range(1, (n, nt)[phase]):
            slot = k - 1 + phase * (n - 1)
            device = ((lax.rem(dp + k, n), tz), (dp, lax.rem(tz + k, nt)))[phase]
            m = remote(
                (stats, stats_mid)[phase].at[which], stats_in.at[which, slot],
                stats_send.at[which, slot], stats_recv.at[which, slot], device,
            )
            m.start()
            stat_msgs[which, slot] = m

    def merged(which, phase):
        mine = (stats, stats_mid)[phase]
        slots = range(phase * (n - 1), phase * (n - 1) + (n, nt)[phase] - 1)
        for slot in slots:
            stat_msgs[which, slot].wait_recv()
        peaks = [mine[which, 0]] + [stats_in[which, slot, 0] for slot in slots]
        totals = [mine[which, 1]] + [stats_in[which, slot, 1] for slot in slots]
        top = functools.reduce(jnp.maximum, peaks)
        return top, sum(t * jnp.exp(p - top) for p, t in zip(peaks, totals))

    def stats_next(which):
        top, total = merged(which, 0)
        stats_mid[which, 0] = top
        stats_mid[which, 1] = total
        stats_out(which, 1)

    def stats_end(which):
        top, total = merged(which, 1)
        scale[which] = (2.0, 1.0)[which] * jnp.exp(stats[which, 0] - top) / total

    steps = (step_a, step_b, step_c, step_d, step_f, step_e)
    needs = ((12,), (13, 16), (14, 17), (15, 18))
    waits = ((0, 1), (2, 3), (4,), ())
    done, held, students = [], None, 0
    for kind, p in PLAN:
        if kind < len(steps):
            steps[kind](p)
            continue
        d = kind - len(steps)
        j = done.count((p, d))
        if j == 0:
            if d == 0:
                for i in waits[p]:
                    loads[i].wait()
            arrived(p, *needs[d])
            peak, total = zero - jnp.inf, zero
        peak, total = logits(p, d, j, peak, total, held)
        done.append((p, d))
        if j < tiles - 1:
            continue
        if held is not None:
            record(held, total)
            students += held[0] == 0
        held = (min(p, 1), d, peak) if p in (0, PIECES - 1) else None
        if students >= 4:
            if students == 4:
                rows_copy = pltpu.make_async_copy(s_rows, rows_out, out_sem.at[4])
                rows_copy.start()
                stats_out(0, 0)
            elif students == 6:
                stats_next(0)
            elif students == 8:
                stats_end(0)
            students += 1
    settle(held)
    for m in id_msgs:
        m.wait()

    def column_of(ref_row):
        return jnp.concatenate([as_column(ref_row(h)) for h in range(2)], axis=0)

    def student_part(d):
        rows = rows_of(d)
        s_scale = column_of(lambda h: scale[0, pl.ds(other(d) * 2 + h, 1), :])
        wanted = column_of(lambda h: ids[other(d) * 2 + h][:1, :])

        def step(j, carry):
            cols = cols_of(j)
            hit = jnp.where(wanted == column_ids(j).astype(jnp.float32), 1.0, 0.0)
            s_exp[rows, cols] = s_exp[rows, cols] * s_scale - hit
            return carry

        lax.fori_loop(0, tiles, step, 0)

    stats_out(1, 0)
    student_part(3)
    student_part(1)
    stats_next(1)
    student_part(2)
    student_part(0)
    stats_end(1)

    tokens = t_rows.shape[0]
    half = depth // 2
    grads = t_w
    outs, pairs, sent = [], {}, {}
    order = (3, 1, 2, 0)

    def teacher_scale(d):
        return column_of(lambda h: scale[1, pl.ds(other(d) * 2 + h, 1), :])

    def gradient(d, j, t_scale):
        rows, cols = rows_of(d), cols_of(j)
        g = s_exp[rows, cols] - t_exp[rows, cols] * t_scale
        grads[rows, cols] = g.astype(jnp.bfloat16)

    def back(d, following, between=None):
        rows = rows_of(d)
        t_scale = None if following is None else teacher_scale(following)

        def step(j, carry):
            cols = cols_of(j)
            t_exp[rows, cols] = lax.dot_general(
                grads[rows, :], s_w[cols, :], (((1,), (1,)), ((), ())), preferred_element_type=jnp.float32
            )
            if following is not None:
                gradient(following, j, t_scale)
            return carry

        if between is None:
            lax.fori_loop(0, tiles, step, 0)
        else:
            lax.fori_loop(0, tiles // 2, step, 0)
            between()
            lax.fori_loop(tiles // 2, tiles, step, 0)
        theirs = pl.ds(pl.multiple_of(other(d) * pair + (1 - core) * block, block), block)
        pairs[d] = remote(t_exp.at[theirs], pair_in.at[d], pair_send.at[d], pair_recv.at[d], sibling)
        pairs[d].start()

    def grads_out(d):
        rows = rows_of(d)
        outs.append(pltpu.make_async_copy(grads.at[rows], grad_out.at[rows], out_sem.at[d]))
        outs[-1].start()

    def own_sum(d, h):
        mine = pl.ds(pl.multiple_of(other(d) * pair + core * block, block), block)
        cols = pl.ds(h * half, half)
        return t_exp[mine, cols] + pair_in[d, :, cols]

    def stage(d, h, value):
        place = grads.at[pl.ds(tokens + (d - 1) * block, block), pl.ds(h * half, half)]
        place[...] = value.astype(jnp.bfloat16)
        return place

    def hop(h):
        sent["hop", h] = remote(
            stage(3, h, own_sum(3, h)), hop_in.at[h], hop_send.at[h], hop_recv.at[h], near[h]
        )
        sent["hop", h].start()

    def plane(d, h, extra):
        value = own_sum(d, h)
        if extra:
            sent["hop", h].wait_recv()
            value = value + hop_in[h].astype(jnp.float32)
        sent[d, h] = remote(
            stage(d, h, value), plane_in.at[d - 1, h],
            plane_send.at[d - 1, h], plane_recv.at[d - 1, h], near[d - 1],
        )
        sent[d, h].start()

    t_scale = teacher_scale(3)

    def first_gradient(j, carry):
        gradient(3, j, t_scale)
        return carry

    lax.fori_loop(0, tiles, first_gradient, 0)
    grads_out(3)
    back(3, 1)
    grads_out(1)
    back(1, 2, lambda: (pairs[3].wait(), hop(0), hop(1)))
    grads_out(2)
    back(2, 0)
    pairs[1].wait()
    plane(1, 0, False)
    grads_out(0)
    back(0, None)
    pairs[2].wait()
    plane(2, 1, False)
    plane(1, 1, True)
    plane(2, 0, True)
    pairs[0].wait()
    for h in range(2):
        s_exp[0:block, pl.ds(h * half, half)] = own_sum(0, h)
    for d, h in ((1, 0), (2, 1), (1, 1), (2, 0)):
        sent[d, h].wait_recv()
        s_exp[0:block, pl.ds(h * half, half)] += plane_in[d - 1, h].astype(jnp.float32)
    for k in range(nt):
        part = pl.ds(pl.multiple_of(lax.rem(tz + k, nt) * features, features), features)
        part_outs[k][...] = s_exp[0:block, part].astype(part_outs[k].dtype)
    for m in sent.values():
        m.wait_send()
    for m in stat_msgs.values():
        m.wait_send()
    for m in msgs.values():
        m.wait_send()
    for copy in outs:
        copy.wait()
    rows_copy.wait()


def head_kernel(rows_ref, grad_ref, out_ref):
    out_ref[...] = lax.dot_general(
        rows_ref[...], grad_ref[...], (((0,), (0,)), ((), ())), preferred_element_type=jnp.float32
    )


def head_gradient(student_rows, logit_grad):
    tokens, depth = student_rows.shape
    width = logit_grad.shape[1]
    strip = depth // 4
    return pl.pallas_call(
        head_kernel,
        grid=(depth // strip,),
        in_specs=[
            pl.BlockSpec((tokens, strip), lambda i: (0, i)),
            pl.BlockSpec((tokens, width), lambda i: (0, 0)),
        ],
        out_specs=pl.BlockSpec((strip, width), lambda i: (i, 0)),
        out_shape=jax.ShapeDtypeStruct((depth, width), jnp.float32),
        compiler_params=pltpu.CompilerParams(vmem_limit_bytes=62 * 1024 * 1024),
        cost_estimate=pl.CostEstimate(
            flops=2 * tokens * depth * width,
            bytes_accessed=2 * tokens * (depth + width) + 4 * depth * width,
            transcendentals=0,
        ),
    )(student_rows, logit_grad)


def fused(n, nt, teacher_hidden, student_hidden, target_ids, teacher_head, student_head):
    block, teacher_depth = teacher_hidden.shape
    depth, width = student_head.shape
    tokens = n * block
    features = depth // nt
    half = depth // 2
    f32, bf16, dma = jnp.float32, jnp.bfloat16, pltpu.SemaphoreType.DMA
    anywhere = pl.BlockSpec(memory_space=pl.ANY)
    whole = pl.BlockSpec(memory_space=pltpu.VMEM)
    swaps = n - 1 + nt - 1
    logit_grad, student_rows, *parts = pl.pallas_call(
        functools.partial(kernel, n, nt, width // 2),
        out_shape=(
            jax.ShapeDtypeStruct((tokens, width), bf16),
            jax.ShapeDtypeStruct((tokens, depth), bf16),
            jax.ShapeDtypeStruct((block, features), f32),
        )
        + (jax.ShapeDtypeStruct((block, features), bf16),) * (nt - 1),
        in_specs=[anywhere, anywhere, whole, anywhere, anywhere],
        out_specs=(anywhere, anywhere) + (whole,) * nt,
        scratch_shapes=[
            pltpu.VMEM((tokens, teacher_depth), bf16),
            pltpu.VMEM((tokens, depth), bf16),
            pltpu.VMEM((n, 8, block), f32),
            pltpu.VMEM((teacher_depth, width), bf16),
            pltpu.VMEM((depth, width), bf16),
            pltpu.VMEM((tokens, width), f32),
            pltpu.VMEM((tokens, width), f32),
            pltpu.VMEM((2, 2, n, block), f32),
            pltpu.VMEM((2, swaps, 2, n, block), f32),
            pltpu.VMEM((2, 2, n, block), f32),
            pltpu.VMEM((2, n, block), f32),
            pltpu.VMEM((n // 2, block, depth), f32),
            pltpu.VMEM((2, block, half), bf16),
            pltpu.VMEM((2, 2, block, half), bf16),
            dma((5,)), dma((5,)),
            dma((PIECES, SLOTS)), dma((PIECES, SLOTS)),
            dma((n - 1,)), dma((n - 1,)),
            dma((2, swaps)), dma((2, swaps)),
            dma((n // 2,)), dma((n // 2,)),
            dma((2,)), dma((2,)),
            dma((2, 2)), dma((2, 2)),
        ],
        compiler_params=pltpu.CompilerParams(
            collective_id=0, has_side_effects=True, vmem_limit_bytes=67043328
        ),
    )(teacher_hidden, student_hidden, target_ids.reshape(1, block), teacher_head, student_head)
    input_grad = parts[0]
    arrived = []
    for k in range(1, nt):
        ring = [(i, (i + k) % nt) for i in range(nt)]
        arrived.append(lax.ppermute(parts[k], "tensor", ring))
    head_grad = head_gradient(student_rows, logit_grad)
    for other in arrived:
        input_grad = input_grad + other.astype(f32)
    return head_grad, input_grad


def choose(n, nt, *arrays):
    teacher_hidden, student_hidden, _, teacher_head, student_head = arrays
    block, width = teacher_hidden.shape[0], student_head.shape[1]
    fits = (
        n == 8
        and nt in (2, 4, 8)
        and block == 128
        and width == student_head.shape[0]
        and teacher_head.shape[0] % 512 == 0
        and width % 512 == 0
        and teacher_head.shape[0] >= n * block + 3 * block
    )
    return fused(n, nt, *arrays) if fits else body(*arrays)


def solution(mesh):
    placed = (
        P("dp", None),
        P("dp", None),
        P("dp"),
        P(None, ("dp", "tensor")),
        P(None, ("dp", "tensor")),
    )
    return jax.shard_map(
        functools.partial(choose, mesh.shape["dp"], mesh.shape["tensor"]),
        mesh=mesh,
        in_specs=placed,
        out_specs=(P(None, ("dp", "tensor")), P("dp", "tensor")),
        check_vma=False,
    )
```
